32 devices in a mesh: wide: 8 (over y, x, core), narrow: 4 (over z).
Axes of the slice: x: 2, y: 2, z: 4, core: 2. Of those that a mesh axis runs over, the one named last changes fastest.
Arguments:
- initial: float32 [2, 256, 128, 128], P(None, 'wide', 'narrow'), may hold values from 0.5 to 2
- images: float32 [2, 4, 24, 24, 128], P(None, None, 'wide', 'narrow'), may hold values from 20 to 200
- blocks: bfloat16 [4, 8, 128, 128], replicated, may hold values from 0 to 0.03125
- lib_index: int32 [4, 256, 128], P(None, 'wide', 'narrow'), may hold values from 0 to 7
- tile_map: int32 [4, 256, 128], P(None, 'wide', 'narrow'), may hold values from 0 to 161
- win_x: int32 [8, 4, 4], P('wide', 'narrow'), may hold values from 0 to 31
- win_y: int32 [8, 4, 4], P('wide', 'narrow'), may hold values from 0 to 31
- win_z: int32 [8, 4, 4], P('wide', 'narrow'), may hold values from 0 to 64
Outputs:
- volume: float32 [2, 256, 128, 128], P(None, 'wide', 'narrow')
- correlation: float32 [8, 4, 4, 4096], P('wide', 'narrow')
The draws below stay inside these ranges and needn't reach their ends.
All inputs are finite; a program needn't handle non-finite values.
Results may differ from the reference program's by a relative error of at most 0.00062.
Values may be sent and summed in bfloat16 or wider, within the bound.
No kernel may reach another device: no remote copies, remote signals or barrier semaphores. Data moves between devices by JAX's collectives and lax.ppermute only.
A program may use at most 128 MiB of HBM per device.

```python
import math
import jax
import jax.numpy as jnp
from jax import lax

CAMS = 4
NLIB = 8
PT = 128
DEPTH = 128
BX = 32
BY = 32
WIN = 64
DISP = 16
SWEEPS = 2
TPR = 3
TPC = 6
WIN_DEV = 4
REACH = 4
BRICKS_X = 8
BRICKS_Y = 4
NX = 256
NY = 128
TROWS = 24
TCOLS = 24
N_WIDE = 8
N_NARROW = 4


def draw_blocks(key, part):
    shape = (CAMS, NLIB, PT, DEPTH)
    uniform_part = jax.random.uniform(key, shape, jnp.float32)
    camera_ids = lax.broadcasted_iota(jnp.int32, shape, 0)
    member_ids = lax.broadcasted_iota(jnp.int32, shape, 1)
    pixel_ids = lax.broadcasted_iota(jnp.int32, shape, 2)
    voxel_ids = lax.broadcasted_iota(jnp.int32, shape, 3)
    offset = voxel_ids * PT // DEPTH + member_ids * (PT // NLIB) + camera_ids * (PT // (2 * CAMS))
    band = (pixel_ids - offset) % PT < PT // 2
    return jnp.where(band, uniform_part * (4.0 / PT), 0.0).astype(jnp.bfloat16)


def place_ends(result, rng, least, largest):
    longest = result.shape.index(max(result.shape))
    spots = []
    for shift in (0, 1):
        where = [jax.random.randint(jax.random.fold_in(rng, axis), (), 0, length) for axis, length in enumerate(result.shape)]
        where[longest] = (where[longest] + shift) % result.shape[longest]
        spots.append(tuple(where))
    return result.at[spots[0]].set(least).at[spots[1]].set(largest)


def steps_of(stream_key, extent, split, low, largest):
    level = 1.0
    for dim, parts in split:
        draws = jax.random.uniform(jax.random.fold_in(jax.random.fold_in(stream_key, 6), dim), (parts,), jnp.float32, low / len(split), largest / len(split))
        level = level * jnp.repeat(jnp.exp(draws), extent[dim] // parts).reshape((-1,) + (1,) * (len(extent) - 1 - dim))
    return level


def setup_inputs(seed: int = 0) -> dict:
    key_of = jax.random.split(jax.random.key(seed), 9)
    initial = jnp.clip(jnp.exp(math.log(2.0) - 1.3862944 * jax.random.uniform(key_of[0], (2, NX, NY, DEPTH), jnp.float32) ** steps_of(key_of[0], (2, NX, NY, DEPTH), ((1, 8), (2, 4)), -0.2, 0.2)), 0.5, 2.0)
    images = jnp.clip(jnp.exp(math.log(200.0) - 2.3025851 * jax.random.uniform(key_of[1], (2, CAMS, TROWS, TCOLS, PT), jnp.float32) ** steps_of(key_of[1], (2, CAMS, TROWS, TCOLS, PT), ((2, 8), (3, 4)), -0.2, 0.2)), 20.0, 200.0)
    blocks = draw_blocks(jax.random.fold_in(key_of[8], 71), 0)
    lib_index = place_ends(jax.random.randint(key_of[3], (CAMS, NX, NY), 0, NLIB), jax.random.fold_in(key_of[3], 1), 0, NLIB - 1).astype(jnp.int32)
    tile_map = place_ends(jax.random.randint(key_of[4], (CAMS, NX, NY), 0, (2 * REACH + 1) * TPR * TPC), jax.random.fold_in(key_of[4], 1), 0, ((2 * REACH + 1) * TPR * TPC) - 1).astype(jnp.int32)
    win_x = place_ends(jax.random.randint(key_of[5], (BRICKS_X, BRICKS_Y, WIN_DEV), 0, BX), jax.random.fold_in(key_of[5], 1), 0, BX - 1).astype(jnp.int32)
    win_y = place_ends(jax.random.randint(key_of[6], (BRICKS_X, BRICKS_Y, WIN_DEV), 0, BY), jax.random.fold_in(key_of[6], 1), 0, BY - 1).astype(jnp.int32)
    win_z = place_ends(jax.random.randint(key_of[7], (BRICKS_X, BRICKS_Y, WIN_DEV), 0, DEPTH - WIN + 1), jax.random.fold_in(key_of[7], 1), 0, DEPTH - WIN).astype(jnp.int32)
    return {"initial": initial, "images": images, "blocks": blocks, "lib_index": lib_index, "tile_map": tile_map, "win_x": win_x, "win_y": win_y, "win_z": win_z}


def column_tiles(rel):
    tile_count = TPR * TPC
    brick_row = (jnp.arange(NX, dtype=jnp.int32) // BX)[:, None]
    brick_col = (jnp.arange(NY, dtype=jnp.int32) // BY)[None, :]
    strip = brick_row - REACH + rel // tile_count
    within = rel % tile_count
    flat = (strip * TPR + within // TPC) * TCOLS + brick_col * TPC + within % TPC
    valid = (strip >= 0) & (strip < N_WIDE)
    return jnp.where(valid, flat, TROWS * TCOLS).astype(jnp.int32)

def reference(initial, images, blocks, lib_index, tile_map, win_x, win_y, win_z):
    volume = initial.astype(jnp.float32)
    tiles_total = TROWS * TCOLS
    logs = jnp.log(images + 1.0).reshape(2, CAMS, tiles_total, PT)
    for sweep_index in range(SWEEPS):
        for camera in range(CAMS):
            target = column_tiles(tile_map[camera]).reshape(-1)
            chosen = lib_index[camera]
            rounded = lax.optimization_barrier(volume.astype(jnp.bfloat16)).astype(jnp.float32)
            column_proj = jnp.zeros((2, NX, NY, PT), jnp.float32)
            for member in range(NLIB):
                weights = blocks[camera, member].astype(jnp.float32)
                product = jnp.einsum('exyk,pk->exyp', rounded, weights)
                column_proj = column_proj + jnp.where((chosen == member)[None, :, :, None], product, 0.0)
            flat_proj = column_proj.reshape(2, NX * NY, PT).transpose(1, 0, 2)
            summed = jax.ops.segment_sum(flat_proj, target, num_segments=tiles_total + 1)
            projection = summed[:tiles_total].transpose(1, 0, 2)
            log_ratio = (logs[:, camera] - jnp.log(projection + 1.0)).astype(jnp.bfloat16)
            padded_ratio = jnp.concatenate([log_ratio, jnp.zeros((2, 1, PT), jnp.bfloat16)], axis=1)
            spread = padded_ratio[:, target].reshape(2, NX, NY, PT).astype(jnp.float32)
            back_sum = jnp.zeros((2, NX, NY, DEPTH), jnp.float32)
            for member in range(NLIB):
                weights = blocks[camera, member].astype(jnp.float32)
                product = jnp.einsum('exyp,pk->exyk', spread, weights)
                back_sum = back_sum + jnp.where((chosen == member)[None, :, :, None], product, 0.0)
            volume = volume * jnp.exp(back_sum)
    half = WIN // 2
    padded = jnp.pad(volume, ((0, 0), (half, half), (half, half), (0, 0)))
    brick_x = (jnp.arange(N_WIDE, dtype=jnp.int32) * BX)[:, None, None]
    brick_y = (jnp.arange(N_NARROW, dtype=jnp.int32) * BY)[None, :, None]
    start_x = (win_x + brick_x).reshape(-1)
    start_y = (win_y + brick_y).reshape(-1)
    start_z = win_z.reshape(-1)
    starts = jnp.stack([start_x, start_y, start_z], axis=1).astype(jnp.int32)
    shifts = (jnp.arange(DISP, dtype=jnp.int32) - DISP // 2) % WIN

    def one_window(start):
        window = lax.dynamic_slice(padded, (jnp.int32(0), start[0], start[1], start[2]), (2, WIN, WIN, WIN))
        centred = window - lax.optimization_barrier(jnp.mean(window, axis=(1, 2, 3), keepdims=True))
        rms = jnp.sqrt(lax.optimization_barrier(jnp.mean(centred * centred, axis=(1, 2, 3))) + 1e-06)
        spectra = jnp.fft.fftn(centred, axes=(1, 2, 3))
        cross = jnp.conj(spectra[0]) * spectra[1]
        circular = jnp.real(jnp.fft.ifftn(cross))
        picked = circular[shifts][:, shifts][:, :, shifts]
        return (picked / (rms[0] * rms[1] * WIN ** 1.5)).reshape(-1)
    correlation = lax.map(one_window, starts).reshape(N_WIDE, N_NARROW, WIN_DEV, DISP * DISP * DISP)
    return (volume, correlation.astype(jnp.float32))
```

```python
import functools
import numpy as np
import jax
import jax.numpy as jnp
from jax import lax
from jax.experimental import pallas as pl
from jax.experimental.pallas import tpu as pltpu
from jax.sharding import PartitionSpec as P

WIN = 64
DISP = 16
SWEEPS = 2
STEPS = 4


def split_table(table):
    high = np.asarray(table, np.float32).astype(jnp.bfloat16)
    low = (np.asarray(table, np.float64) - high.astype(np.float64)).astype(np.float32)
    return high, low.astype(jnp.bfloat16)


def window_tables():
    half = WIN // 2 + 1
    unit = 2.0 * np.pi / WIN
    index = np.arange(WIN)
    shifts = np.arange(DISP) - DISP // 2
    turn = unit * np.outer(index, index)
    cos_full, sin_full = np.cos(turn), np.sin(turn)
    rows_y = -(-2 * half // 8) * 8
    first = np.zeros((rows_y, WIN))
    first[0 : 2 * half : 2] = cos_full[:half]
    first[1 : 2 * half : 2] = -sin_full[:half]
    high, low = split_table(first)
    table_y = np.concatenate([high, high, low], axis=1)
    second = np.block([[cos_full, sin_full], [-sin_full, cos_full]])
    high, low = split_table(second)
    table_x = np.concatenate([high, high, low], axis=1)
    third = np.zeros((2, 2, WIN, 2, 2, WIN))
    for e in range(2):
        third[0, e, :, e, 0] = cos_full
        third[1, e, :, e, 0] = sin_full
        third[0, e, :, e, 1] = -sin_full
        third[1, e, :, e, 1] = cos_full
    table_z = np.stack(split_table(third.reshape(4 * WIN, 4 * WIN)))
    part = unit * np.outer(index, shifts)
    cos_part, sin_part = np.cos(part), np.sin(part)
    fourth = np.zeros((4, WIN, 4 * WIN))
    real = np.stack([cos_part, cos_part, -sin_part, sin_part])
    imag = np.stack([sin_part, sin_part, cos_part, -cos_part])
    fourth[..., 0:DISP] = real
    fourth[..., DISP : 2 * DISP] = imag
    fourth[..., 2 * WIN : 2 * WIN + DISP] = -imag
    fourth[..., 2 * WIN + DISP : 2 * WIN + 2 * DISP] = real
    table_iz = np.stack(split_table(fourth.reshape(4 * WIN, 4 * WIN)))
    high, low = split_table(np.concatenate([cos_part.T, sin_part.T], axis=1))
    table_ix = np.concatenate([high, high, low], axis=1)
    weight = np.full(half, 2.0)
    weight[0] = weight[-1] = 1.0
    pad = -(-half // 16) * 16
    last = np.zeros((2 * DISP, pad))
    last[:DISP, :half] = cos_part.T[:, :half] * weight
    last[DISP:, :half] = sin_part.T[:, :half] * weight
    high, low = split_table(last)
    table_iy = np.concatenate([high, high, low], axis=1)
    return table_y, table_x, table_z, table_iz, table_ix, table_iy


def halves(value):
    high = value.astype(jnp.bfloat16)
    low = (value - high.astype(jnp.float32)).astype(jnp.bfloat16)
    return high, low


def stacked(value):
    high, low = halves(value)
    return jnp.concatenate([high, low, high], axis=0)


def mul(left, right):
    return jnp.dot(left, right, preferred_element_type=jnp.float32)


def window_body(count, starts, *refs):
    bricks = refs[:9]
    t_y, t_x, t_z, t_iz, t_ix, t_iy, out = refs[9:16]
    ext, sems, folded, spectrum, high_ref, low_ref, product, turned = refs[16:]
    half_win = WIN // 2
    half = WIN // 2 + 1
    rows_y = t_y.shape[0]
    pad = t_iy.shape[1] // 3
    copies = [
        pltpu.make_async_copy(bricks[i], ext.at[i // 3, i % 3], sems.at[i]) for i in range(9)
    ]
    for copy in copies:
        copy.start()
    product[...] = jnp.zeros_like(product)
    turned[...] = jnp.zeros_like(turned)
    for copy in copies:
        copy.wait()
    lane = lax.broadcasted_iota(jnp.int32, (WIN, 2 * WIN), 1)
    row = lax.broadcasted_iota(jnp.int32, (half_win, 2 * WIN), 0)
    left_lane = lane < WIN
    left_row = left_lane[:1]

    def one_window(w, carry):
        sx, sy, sz = starts[w, 0], starts[w, 1], starts[w, 2]
        keep = (left_lane & (lane >= sz)) | (~left_lane & (lane < sz + WIN))
        near = row >= sy

        def fold(i, total):
            for j in range(8):
                x = i * 8 + j
                brick = jnp.where(x >= half_win, 1, jnp.where(x >= sx, 0, 2))
                inner = x & (half_win - 1)
                values = []
                for e in range(2):
                    low = ext[brick, 0, e, inner]
                    own = ext[brick, 1, e, inner]
                    high = ext[brick, 2, e, inner]
                    values.append(jnp.concatenate([jnp.where(near, low, high), own], axis=0))
                stay = jnp.where(left_lane, values[0], values[1])
                move = jnp.where(left_lane, values[1], values[0])
                value = jnp.where(keep, stay, pltpu.roll(move, WIN, 1))
                folded[x] = value
                total = total + value
            return total

        total = lax.fori_loop(0, WIN // 8, fold, jnp.zeros((WIN, 2 * WIN), jnp.float32))
        total = jnp.sum(total, axis=0, keepdims=True)
        scale = 1.0 / WIN**3
        mean = jnp.where(
            left_row,
            jnp.sum(jnp.where(left_row, total, 0.0), axis=1, keepdims=True) * scale,
            jnp.sum(jnp.where(left_row, 0.0, total), axis=1, keepdims=True) * scale,
        )

        def first(i, square):
            for j in range(8):
                x = i * 8 + j
                value = folded[x] - mean
                square = square + value * value
                result = mul(t_y[...], stacked(value))
                spectrum[pl.ds(x, rows_y, stride=WIN), :] = result
            return square

        square = lax.fori_loop(0, WIN // 8, first, jnp.zeros((WIN, 2 * WIN), jnp.float32))
        square = jnp.sum(square, axis=0, keepdims=True)
        power_0 = jnp.sum(jnp.where(left_row, square, 0.0), axis=1, keepdims=True) * scale
        power_1 = jnp.sum(jnp.where(left_row, 0.0, square), axis=1, keepdims=True) * scale
        norm = jnp.sqrt(power_0 + 1e-06) * jnp.sqrt(power_1 + 1e-06)
        factor = 1.0 / (WIN**3 * WIN**1.5) / norm

        def second(i, done):
            for j in range(11):
                k = i * 11 + j
                start = pl.multiple_of(k * 2 * WIN, 2 * WIN)
                value = spectrum[pl.ds(start, 2 * WIN), :]
                result = mul(t_x[...], stacked(value))
                result = jnp.concatenate([result[:WIN], result[WIN:]], axis=1)
                high, low = halves(result)
                place = pl.multiple_of(k * WIN, WIN)
                high_ref[pl.ds(place, WIN), :] = high
                low_ref[pl.ds(place, WIN), :] = low
            return done

        lax.fori_loop(0, half // 11, second, 0)
        block = half * WIN // 6

        def third(i, done):
            place = pl.ds(pl.multiple_of(i * block, block), block)
            high, low = high_ref[place, :], low_ref[place, :]
            value = mul(high, t_z[0]) + mul(low, t_z[0]) + mul(high, t_z[1])
            one, two = value[:, : 2 * WIN] * factor, value[:, 2 * WIN :]
            cross = jnp.concatenate([one * two, one * pltpu.roll(two, WIN, 1)], axis=1)
            high, low = halves(cross)
            value = mul(high, t_iz[0]) + mul(low, t_iz[0]) + mul(high, t_iz[1])
            shift = w * (2 * DISP)
            product[place, : 2 * WIN] += pltpu.roll(value[:, : 2 * WIN], shift, 1)
            product[place, 2 * WIN :] += pltpu.roll(value[:, 2 * WIN :], shift, 1)
            return done

        lax.fori_loop(0, 6, third, 0)
        return carry

    lax.fori_loop(0, count, one_window, 0)

    def fifth(i, done):
        for j in range(11):
            k = i * 11 + j
            value = product[pl.ds(pl.multiple_of(k * WIN, WIN), WIN), :]
            value = jnp.concatenate([value[:, : 2 * WIN], value[:, 2 * WIN :]], axis=0)
            turned[pl.ds(k, DISP, stride=pad), :] = mul(t_ix[...], stacked(value))
        return done

    lax.fori_loop(0, half // 11, fifth, 0)
    for d in range(DISP):
        value = mul(t_iy[...], stacked(turned[d * pad : (d + 1) * pad, :]))
        out[:, d * 2 * WIN : (d + 1) * 2 * WIN] = value[:DISP] - pltpu.roll(
            value[DISP:], 2 * WIN - DISP, 1
        )


def window_correlations(bricks, starts):
    count = starts.shape[0]
    tables = window_tables()
    half = WIN // 2 + 1
    rows_y = tables[0].shape[0]
    pad = tables[5].shape[1] // 3
    brick = bricks[0].shape
    vmem = pl.BlockSpec(memory_space=pltpu.VMEM)
    result = pl.pallas_call(
        functools.partial(window_body, count),
        out_shape=jax.ShapeDtypeStruct((DISP, DISP * 2 * WIN), jnp.float32),
        in_specs=[pl.BlockSpec(memory_space=pltpu.SMEM)]
        + [pl.BlockSpec(memory_space=pl.ANY)] * 9
        + [vmem] * 6,
        out_specs=vmem,
        scratch_shapes=[
            pltpu.VMEM((3, 3) + brick, jnp.float32),
            pltpu.SemaphoreType.DMA((9,)),
            pltpu.VMEM((WIN, WIN, 2 * WIN), jnp.float32),
            pltpu.VMEM((rows_y * WIN, 2 * WIN), jnp.float32),
            pltpu.VMEM((half * WIN, 4 * WIN), jnp.bfloat16),
            pltpu.VMEM((half * WIN, 4 * WIN), jnp.bfloat16),
            pltpu.VMEM((half * WIN, 4 * WIN), jnp.float32),
            pltpu.VMEM((DISP * pad, 2 * WIN), jnp.float32),
        ],
        name="windows",
    )(starts, *bricks, *[jnp.asarray(t) for t in tables])
    result = result.reshape(DISP, DISP, 2 * WIN // (2 * DISP), 2 * DISP)[:, :, :count, :DISP]
    return result.transpose(2, 1, 0, 3).reshape(count, DISP**3)


LANES = 128


def tree_sum(values):
    while len(values) > 1:
        values = [sum(values[i : i + 2]) for i in range(0, len(values), 2)]
    return values[0]


def chosen_products(value, member, weights_ref):
    count = weights_ref.shape[1]
    low_count = count // 2
    size = weights_ref.shape[2]
    terms = []
    for start in range(0, low_count, 2):
        picked, tables = [], []
        for j in range(start, min(start + 2, low_count)):
            hit = (member == j) | (member == j + low_count)
            picked.append(jnp.where(hit, value, 0.0).astype(jnp.bfloat16))
            tables.append(
                jnp.concatenate([weights_ref[0, j], weights_ref[0, j + low_count]], axis=1)
            )
        terms.append(mul(jnp.concatenate(picked, axis=1), jnp.concatenate(tables, axis=0)))
    both = tree_sum(terms)
    return jnp.where(member < low_count, both[:, :size], both[:, size:])


def sweep_body(back, forward, *refs):
    refs = list(refs)
    volume_ref = refs.pop(0)
    if back:
        ratio_ref, back_code, back_weights = refs[:3]
        refs = refs[3:]
    if forward:
        next_code, next_row, next_weights = refs[:3]
        refs = refs[3:]
    if back:
        volume_out = refs.pop(0)
    if forward:
        partial_ref = refs.pop(0)
    exposures, block, depth = volume_ref.shape
    member_count = back_weights.shape[1] if back else next_weights.shape[1]
    volumes = [volume_ref[e] for e in range(exposures)]
    if back:
        code = back_code[0]
        tile, member = code // member_count, code % member_count
        tiles = ratio_ref.shape[1]
        padded = -(-tiles // LANES) * LANES
        columns = lax.broadcasted_iota(jnp.int32, (block, LANES), 1)
        placement = jnp.concatenate(
            [
                jnp.where(tile == columns + start, 1.0, 0.0).astype(jnp.bfloat16)
                for start in range(0, padded, LANES)
            ],
            axis=1,
        )[:, :tiles]
        ratios = jnp.concatenate([ratio_ref[e] for e in range(exposures)], axis=1)
        spread = mul(placement, ratios)
        for e in range(exposures):
            part = spread[:, e * LANES : (e + 1) * LANES]
            volumes[e] = volumes[e] * jnp.exp(chosen_products(part, member, back_weights))
            volume_out[e] = volumes[e]
    if forward:
        code = next_code[0]
        member = code % member_count
        tiles = partial_ref.shape[1]
        parts = []
        for e in range(exposures):
            rounded = volumes[e].astype(jnp.bfloat16).astype(jnp.float32)
            parts.extend(halves(chosen_products(rounded, member, next_weights)))
        rows = lax.broadcasted_iota(jnp.int32, (tiles, block), 0)
        placement = jnp.where(next_row[0] // member_count == rows, 1.0, 0.0).astype(jnp.bfloat16)
        value = mul(placement, jnp.concatenate(parts, axis=1))
        size = value.shape[1] // (2 * exposures)
        first = pl.program_id(0) == 0
        for e in range(exposures):
            start = 2 * e * size
            total = value[:, start : start + size] + value[:, start + size : start + 2 * size]

            @pl.when(first)
            def _():
                partial_ref[e] = total

            @pl.when(jnp.logical_not(first))
            def _():
                partial_ref[e] += total


def sweep_step(volume, ratio, codes, rows, weights, weights_turned, tiles, camera, following):
    exposures, columns, depth = volume.shape
    members, pixels = weights.shape[1], weights.shape[2]
    block = columns // STEPS
    back, forward = camera is not None, following is not None

    def fixed(shape, place):
        return pl.BlockSpec(shape, lambda i: place)

    def code_spec(index):
        return pl.BlockSpec((1, block, LANES), lambda i: (index, i, 0))

    volume_spec = pl.BlockSpec((exposures, block, depth), lambda i: (0, i, 0))
    operands, specs, shapes, outs = [volume], [volume_spec], [], []
    if back:
        operands += [ratio, codes, weights]
        specs += [
            fixed(ratio.shape, (0, 0, 0)),
            code_spec(camera),
            fixed((1,) + weights.shape[1:], (camera, 0, 0, 0)),
        ]
        shapes.append(jax.ShapeDtypeStruct(volume.shape, jnp.float32))
        outs.append(volume_spec)
    if forward:
        operands += [codes, rows, weights_turned]
        specs += [
            code_spec(following),
            pl.BlockSpec((1, 1, block), lambda i: (following, 0, i)),
            fixed((1,) + weights_turned.shape[1:], (following, 0, 0, 0)),
        ]
        shapes.append(jax.ShapeDtypeStruct((exposures, tiles, pixels), jnp.float32))
        outs.append(fixed((exposures, tiles, pixels), (0, 0, 0)))
    result = pl.pallas_call(
        functools.partial(sweep_body, back, forward),
        grid=(STEPS,),
        in_specs=specs,
        out_specs=outs,
        out_shape=shapes,
        name="sweep",
    )(*operands)
    return (result[0] if back else volume), (result[-1] if forward else None)


def partner_of(count, bit):
    return [(i, i ^ bit) for i in range(count)]


def shared_ratio(partial_value, picture, own_index):
    count = lax.axis_size("wide")
    parity = own_index % 2
    pair = partner_of(count, 1)
    kept = lax.dynamic_index_in_dim(partial_value, parity, 0, keepdims=False)
    sent = lax.dynamic_index_in_dim(partial_value, 1 - parity, 0, keepdims=False)
    total = kept + lax.ppermute(sent, "wide", pair)
    bit = 2
    while bit < count:
        total = total + lax.ppermute(total, "wide", partner_of(count, bit))
        bit *= 2
    ratio = (picture - jnp.log(total + 1.0)).astype(jnp.bfloat16)
    other = lax.ppermute(ratio, "wide", pair)
    odd = parity == 1
    return jnp.stack([jnp.where(odd, other, ratio), jnp.where(odd, ratio, other)])


def reconstructed(initial, images, blocks, lib_index, tile_map):
    count = lax.axis_size("wide")
    own_index = lax.axis_index("wide")
    exposures, brick_x, brick_y, depth = initial.shape
    cameras, tile_rows, tile_cols, pixels = images.shape[1:]
    tile_count = tile_rows * tile_cols
    tiles = count * tile_count
    columns = brick_x * brick_y
    members = blocks.shape[1]
    strip = own_index - count // 2 + tile_map // tile_count
    target = strip * tile_count + tile_map % tile_count
    missing = -(-tiles // LANES) * LANES
    target = jnp.where((strip >= 0) & (strip < count), target, missing)
    codes = (target * members + lib_index).reshape(cameras, columns)
    rows = codes[:, None, :]
    codes = jnp.broadcast_to(codes[:, :, None], (cameras, columns, LANES))
    parity = own_index % 2
    pictures = jnp.log(images.reshape(exposures, cameras, tile_count, pixels) + 1.0)
    by_core = jnp.broadcast_to(pictures[None], (count // 2,) + pictures.shape)
    by_core = by_core.reshape((count, cameras, tile_count, pixels))
    gathered = lax.all_to_all(by_core, "wide", split_axis=0, concat_axis=0, tiled=True)
    gathered = gathered.transpose(1, 0, 2, 3).reshape(cameras, tiles, pixels)
    turned = blocks.transpose(0, 1, 3, 2)
    volume = initial.reshape(exposures, columns, depth)
    order = [camera for _ in range(SWEEPS) for camera in range(cameras)]
    step = functools.partial(
        sweep_step, codes=codes, rows=rows, weights=blocks, weights_turned=turned, tiles=tiles
    )
    volume, partial_value = step(volume, None, camera=None, following=order[0])
    for place, camera in enumerate(order):
        following = order[place + 1] if place + 1 < len(order) else None
        ratio = shared_ratio(partial_value, gathered[camera], own_index)
        volume, partial_value = step(volume, ratio, camera=camera, following=following)
    return volume.reshape(initial.shape)


def neighbours(block):
    def shifted(value, axis, step):
        count = lax.axis_size(axis)
        pairs = [(i, i + step) for i in range(count) if 0 <= i + step < count]
        return lax.ppermute(value, axis, pairs)

    left, right = shifted(block, "wide", 1), shifted(block, "wide", -1)
    near, far = shifted(block, "narrow", 1), shifted(block, "narrow", -1)
    left_near, left_far = shifted(near, "wide", 1), shifted(far, "wide", 1)
    right_near, right_far = shifted(right, "narrow", 1), shifted(right, "narrow", -1)
    return [left_near, left, left_far, near, block, far, right_near, right, right_far]


def body(initial, images, blocks, lib_index, tile_map, win_x, win_y, win_z):
    volume = reconstructed(initial, images, blocks, lib_index, tile_map)
    starts = jnp.stack([win_x.reshape(-1), win_y.reshape(-1), win_z.reshape(-1)], axis=1)
    correlation = window_correlations(neighbours(volume), starts)
    return (volume, correlation.reshape(1, 1, starts.shape[0], DISP * DISP * DISP))


def solution(mesh):
    placed = (
        P(None, "wide", "narrow", None),
        P(None, None, "wide", "narrow", None),
        P(),
        P(None, "wide", "narrow"),
        P(None, "wide", "narrow"),
        P("wide", "narrow", None),
        P("wide", "narrow", None),
        P("wide", "narrow", None),
    )
    return jax.shard_map(
        body,
        mesh=mesh,
        in_specs=placed,
        out_specs=(P(None, "wide", "narrow", None), P("wide", "narrow", None, None)),
        check_vma=False,
    )
```

```python
import functools
import numpy as np
import jax
import jax.numpy as jnp
from jax import lax
from jax.experimental import pallas as pl
from jax.experimental.pallas import tpu as pltpu
from jax.sharding import PartitionSpec as P

WIN = 64
DISP = 16
SWEEPS = 2
TERMS = 4
LEVELS = 65535.0
MIDDLE = 32768.0
GRAIN = 16.0
SPARE = 16
STEPS = 1
FOLD = 16
GROUPS = 2
THIRD = 1
SPLIT = 4


def split_table(table):
    high = np.asarray(table, np.float32).astype(jnp.bfloat16)
    low = (np.asarray(table, np.float64) - high.astype(np.float64)).astype(np.float32)
    return high, low.astype(jnp.bfloat16)


def window_tables(count):
    half = WIN // 2 + 1
    unit = 2.0 * np.pi / WIN
    index = np.arange(WIN)
    shifts = np.arange(DISP) - DISP // 2
    turn = unit * np.outer(index, index)
    cos_full, sin_full = np.cos(turn), np.sin(turn)
    rows_y = -(-2 * half // 8) * 8
    first = np.zeros((rows_y, WIN))
    first[0 : 2 * half : 2] = cos_full[:half]
    first[1 : 2 * half : 2] = -sin_full[:half]
    high, low = split_table(first)
    table_y = np.concatenate([high, high, low], axis=1)
    second = np.block([[cos_full, sin_full], [-sin_full, cos_full]])
    high, low = split_table(second)
    table_x = np.concatenate([high, high, low], axis=1)
    third = np.zeros((2, 2, WIN, 2, 2, WIN))
    for e in range(2):
        third[0, e, :, e, 0] = cos_full
        third[1, e, :, e, 0] = sin_full
        third[0, e, :, e, 1] = -sin_full
        third[1, e, :, e, 1] = cos_full
    high, low = split_table(third.reshape(4 * WIN, 4 * WIN))
    table_z = np.concatenate([high, high, low], axis=0)
    part = unit * np.outer(index, shifts)
    cos_part, sin_part = np.cos(part), np.sin(part)
    fourth = np.zeros((4, WIN, 2 * WIN))
    fourth[..., :DISP] = np.stack([cos_part, cos_part, -sin_part, sin_part])
    fourth[..., DISP : 2 * DISP] = np.stack([sin_part, sin_part, cos_part, -cos_part])
    fourth = fourth.reshape(4 * WIN, 2 * WIN)
    shifted = np.stack([np.roll(fourth, w * 2 * DISP, axis=1) for w in range(count)])
    high, low = split_table(shifted)
    table_iz = np.concatenate([high, high, low], axis=1)
    high, low = split_table(np.concatenate([cos_part.T, sin_part.T], axis=1))
    table_ix = np.concatenate([high, high, low], axis=1)
    weight = np.full(half, 2.0)
    weight[0] = weight[-1] = 1.0
    pad = -(-half // 16) * 16
    last = np.zeros((2 * DISP, pad))
    last[:DISP, :half] = cos_part.T[:, :half] * weight
    last[DISP:, :half] = sin_part.T[:, :half] * weight
    high, low = split_table(last)
    table_iy = np.concatenate([high, high, low], axis=1)
    return table_y, table_x, table_z, table_iz, table_ix, table_iy


def halves(value):
    high = value.astype(jnp.bfloat16)
    low = (value - high.astype(jnp.float32)).astype(jnp.bfloat16)
    return high, low


def stacked(value):
    high, low = halves(value)
    return jnp.concatenate([high, low, high], axis=0)


def mul(left, right):
    return jnp.dot(left, right, preferred_element_type=jnp.float32)


def window_body(count, starts, *refs):
    own, left, right, near, far, left_pair, right_near, right_far = refs[:8]
    t_y, t_x, t_z, t_iz, t_ix, t_iy, out = refs[8:15]
    ext, levels, sems, folded, spectrum, high_ref, low_ref, product, turned = refs[15:]
    half_win = WIN // 2
    half = WIN // 2 + 1
    rows_y = t_y.shape[0]
    pad = t_iy.shape[1] // 3
    sources = [left_pair.at[0], left, left_pair.at[1], near, far, right_near, right, right_far]
    copies = [
        pltpu.make_async_copy(source, levels.at[i], sems.at[i])
        for i, source in enumerate(sources)
    ]
    copies.append(pltpu.make_async_copy(own, ext.at[len(sources) // 2], sems.at[len(sources)]))
    for copy in copies:
        copy.start()
    product[...] = jnp.zeros_like(product)
    turned[...] = jnp.zeros_like(turned)
    for copy in copies:
        copy.wait()
    exposures, columns = ext.shape[1:3]

    def decode(i, done):
        brick = jnp.where(i < len(sources) // 2, i, i + 1)
        for e in range(exposures):
            scale = levels[i, e, columns:, :].astype(jnp.int32).astype(jnp.float32)
            least, width = scale[:1] / GRAIN, scale[1:2]
            step = width / (GRAIN * LEVELS)
            base = least + MIDDLE * step
            present = jnp.where(width > 0.0, 1.0, 0.0)
            for start in range(0, columns, columns // 4):
                place = slice(start, start + columns // 4)
                level = levels[i, e, place, :].astype(jnp.int32).astype(jnp.float32)
                ext[brick, e, place, :] = jnp.exp(level * step + base) * present
        return done

    lax.fori_loop(0, len(sources), decode, 0)
    lane = lax.broadcasted_iota(jnp.int32, (WIN, 2 * WIN), 1)
    row = lax.broadcasted_iota(jnp.int32, (half_win, 2 * WIN), 0)
    left_lane = lane < WIN
    left_row = left_lane[:1]

    def one_window(w, carry):
        sx, sy, sz = starts[w, 0], starts[w, 1], starts[w, 2]
        keep = (left_lane & (lane >= sz)) | (~left_lane & (lane < sz + WIN))
        below = row >= sy

        def fold(i, total):
            for j in range(FOLD):
                x = i * FOLD + j
                brick = jnp.where(x >= half_win, 3, jnp.where(x >= sx, 0, 6))
                inner = pl.ds(pl.multiple_of((x & (half_win - 1)) * half_win, half_win), half_win)
                values = []
                for e in range(2):
                    low = ext[brick + 0, e, inner]
                    same = ext[brick + 1, e, inner]
                    high = ext[brick + 2, e, inner]
                    values.append(jnp.concatenate([jnp.where(below, low, high), same], axis=0))
                stay = jnp.where(left_lane, values[0], values[1])
                move = jnp.where(left_lane, values[1], values[0])
                value = jnp.where(keep, stay, pltpu.roll(move, WIN, 1))
                folded[x] = value
                total = total + value
            return total

        total = lax.fori_loop(0, WIN // FOLD, fold, jnp.zeros((WIN, 2 * WIN), jnp.float32))
        total = jnp.sum(total, axis=0, keepdims=True)
        scale = 1.0 / WIN**3
        mean = jnp.where(
            left_row,
            jnp.sum(jnp.where(left_row, total, 0.0), axis=1, keepdims=True) * scale,
            jnp.sum(jnp.where(left_row, 0.0, total), axis=1, keepdims=True) * scale,
        )

        def first(i, square):
            for g in range(GROUPS):
                start = (i * GROUPS + g) * 8
                results = []
                for j in range(0, 8, 2):
                    values = [folded[start + j + k] - mean for k in range(2)]
                    for value in values:
                        square = square + value * value
                    result = mul(t_y[...], stacked(jnp.concatenate(values, axis=1)))
                    results += [result[:, : 2 * WIN], result[:, 2 * WIN :]]
                spectrum[:, pl.ds(pl.multiple_of(start, 8), 8), :] = jnp.swapaxes(
                    jnp.stack(results), 0, 1
                )
            return square

        square = lax.fori_loop(0, WIN // (8 * GROUPS), first, jnp.zeros((WIN, 2 * WIN), jnp.float32))
        square = jnp.sum(square, axis=0, keepdims=True)
        power_0 = jnp.sum(jnp.where(left_row, square, 0.0), axis=1, keepdims=True) * scale
        power_1 = jnp.sum(jnp.where(left_row, 0.0, square), axis=1, keepdims=True) * scale
        norm = jnp.sqrt(power_0 + 1e-06) * jnp.sqrt(power_1 + 1e-06)
        factor = 1.0 / (WIN**3 * WIN**1.5) / norm

        def second(i, done):
            for j in range(0, 11, 2):
                width = min(2, 11 - j)
                k = i * 11 + j
                values = [
                    spectrum[pl.ds(2 * (k + n), 2)].reshape(2 * WIN, 2 * WIN) for n in range(width)
                ]
                result = mul(t_x[...], stacked(jnp.concatenate(values, axis=1)))
                for n in range(width):
                    part = result[:, 2 * WIN * n : 2 * WIN * (n + 1)]
                    part = jnp.concatenate([part[:WIN], part[WIN:]], axis=1)
                    place = pl.ds(pl.multiple_of((k + n) * WIN, WIN), WIN)
                    high_ref[place, :], low_ref[place, :] = halves(part)
            return done

        lax.fori_loop(0, half // 11, second, 0)
        block = half * WIN // (THIRD * SPLIT)

        def third(i, done):
            for g in range(SPLIT):
                place = pl.ds(pl.multiple_of((i * SPLIT + g) * block, block), block)
                high, low = high_ref[place, :], low_ref[place, :]
                value = mul(jnp.concatenate([high, low, high], axis=1), t_z[...])
                one, two = value[:, : 2 * WIN] * factor, value[:, 2 * WIN :]
                cross = jnp.concatenate([one * two, one * pltpu.roll(two, WIN, 1)], axis=1)
                high, low = halves(cross)
                product[place, :] += mul(jnp.concatenate([high, low, high], axis=1), t_iz[w])
            return done

        lax.fori_loop(0, THIRD, third, 0)
        return carry

    lax.fori_loop(0, count, one_window, 0)

    real_lane = lane % (2 * DISP) < DISP

    def fifth(i, done):
        for j in range(11):
            k = i * 11 + j
            value = product[pl.ds(pl.multiple_of(k * WIN, WIN), WIN), :]
            turn = jnp.where(
                real_lane, -pltpu.roll(value, 2 * WIN - DISP, 1), pltpu.roll(value, DISP, 1)
            )
            value = jnp.concatenate([value, turn], axis=0)
            turned[pl.ds(k, DISP, stride=pad), :] = mul(t_ix[...], stacked(value))
        return done

    lax.fori_loop(0, half // 11, fifth, 0)
    for d in range(DISP):
        value = mul(t_iy[...], stacked(turned[d * pad : (d + 1) * pad, :]))
        out[:, d * 2 * WIN : (d + 1) * 2 * WIN] = value[:DISP] - pltpu.roll(
            value[DISP:], 2 * WIN - DISP, 1
        )


def window_correlations(own, bricks, starts):
    count = starts.shape[0]
    tables = window_tables(count)
    half = WIN // 2 + 1
    rows_y = tables[0].shape[0]
    pad = tables[5].shape[1] // 3
    spread = bricks[0].shape
    vmem = pl.BlockSpec(memory_space=pltpu.VMEM)
    result = pl.pallas_call(
        functools.partial(window_body, count),
        out_shape=jax.ShapeDtypeStruct((DISP, DISP * 2 * WIN), jnp.float32),
        in_specs=[pl.BlockSpec(memory_space=pltpu.SMEM)]
        + [pl.BlockSpec(memory_space=pl.ANY)] * 8
        + [vmem] * 6,
        out_specs=vmem,
        scratch_shapes=[
            pltpu.VMEM((9,) + own.shape, jnp.float32),
            pltpu.VMEM((8,) + spread, jnp.int16),
            pltpu.SemaphoreType.DMA((9,)),
            pltpu.VMEM((WIN, WIN, 2 * WIN), jnp.float32),
            pltpu.VMEM((rows_y, WIN, 2 * WIN), jnp.float32),
            pltpu.VMEM((half * WIN, 4 * WIN), jnp.bfloat16),
            pltpu.VMEM((half * WIN, 4 * WIN), jnp.bfloat16),
            pltpu.VMEM((half * WIN, 2 * WIN), jnp.float32),
            pltpu.VMEM((DISP * pad, 2 * WIN), jnp.float32),
        ],
        name="windows",
    )(starts, own, *bricks, *[jnp.asarray(t) for t in tables])
    result = result.reshape(DISP, DISP, 2 * WIN // (2 * DISP), 2 * DISP)[:, :, :count, :DISP]
    return result.transpose(2, 1, 0, 3).reshape(count, DISP**3)


LANES = 128


def chosen_products(value, member, weights_ref):
    count = weights_ref.shape[1]
    half_count = count // 2
    size = weights_ref.shape[2]
    copies = value.shape[0] // member.shape[0]
    total = None
    for start in range(0, half_count, TERMS):
        picked, tables = [], []
        for j in range(start, min(start + TERMS, half_count)):
            hit = (member == j) | (member == j + half_count)
            hit = jnp.concatenate([hit] * copies, axis=0)
            picked.append(jnp.where(hit, value, jnp.zeros_like(value)))
            tables.append(
                jnp.concatenate([weights_ref[0, j], weights_ref[0, j + half_count]], axis=1)
            )
        term = mul(jnp.concatenate(picked, axis=1), jnp.concatenate(tables, axis=0))
        total = term if total is None else total + term
    upper = jnp.concatenate([member.astype(jnp.float32)] * copies, axis=0) >= half_count
    return jnp.where(upper, total[:, size:], total[:, :size])


def placed_tiles(tile, count):
    columns = lax.broadcasted_iota(jnp.int32, tile.shape, 1).astype(jnp.float32)
    columns = columns.astype(tile.dtype)
    one, zero = jnp.ones_like(tile), jnp.zeros_like(tile)
    parts = [
        jnp.where(tile - start == columns, one, zero) for start in range(0, count, LANES)
    ]
    return jnp.concatenate(parts, axis=1)[:, :count]


def sweep_body(back, forward, parity_ref, *refs):
    refs = list(refs)
    volume_ref = refs.pop(0)
    if back:
        own_ratio, other_ratio, back_tile, back_member, back_weights = refs[:5]
        refs = refs[5:]
    if forward:
        next_row, next_member, next_weights = refs[:3]
        refs = refs[3:]
    if back:
        volume_out = refs.pop(0)
    if forward:
        kept_ref, sent_ref = refs
    exposures, block, depth = volume_ref.shape
    odd = parity_ref[0] == 1
    volume = volume_ref[...].reshape(exposures * block, depth)
    if back:
        own, other = own_ratio[...], other_ratio[...]
        ratios = [jnp.where(odd, other, own), jnp.where(odd, own, other)]
        placement = placed_tiles(back_tile[0], own.shape[0])
        spread = mul(placement, jnp.concatenate(ratios, axis=1)).astype(jnp.bfloat16)
        spread = jnp.concatenate(
            [spread[:, e * LANES : (e + 1) * LANES] for e in range(exposures)], axis=0
        )
        volume = volume * jnp.exp(chosen_products(spread, back_member[0], back_weights))
        volume_out[...] = volume.reshape(exposures, block, depth)
    if not forward:
        (code_ref,) = refs
        for e in range(exposures):
            logs = jnp.log(jnp.maximum(volume[e * block : (e + 1) * block], 1e-37))
            least = jnp.floor(jnp.min(logs, axis=0, keepdims=True) * GRAIN)
            width = jnp.floor(jnp.max(logs, axis=0, keepdims=True) * GRAIN - least) + 1.0
            rate = (GRAIN * LEVELS) / width
            level = jnp.floor((logs - least / GRAIN) * rate + 0.5) - MIDDLE
            code_ref[e, :block, :] = level.astype(jnp.int32).astype(jnp.int16)
            row = lax.broadcasted_iota(jnp.int32, (SPARE, depth), 0)
            extra = jnp.where(row == 0, least, jnp.where(row == 1, width, 0.0))
            code_ref[e, block:, :] = extra.astype(jnp.int32).astype(jnp.int16)
    if forward:
        tiles = kept_ref.shape[0]
        projected = chosen_products(volume.astype(jnp.bfloat16), next_member[0], next_weights)
        parts = list(halves(projected))
        parts = [p[e * block : (e + 1) * block] for p in parts for e in range(exposures)]
        rows = lax.broadcasted_iota(jnp.int32, (tiles, block), 0)
        placement = jnp.where(next_row[0] == rows, 1.0, 0.0).astype(jnp.bfloat16)
        value = mul(placement, jnp.concatenate(parts, axis=1))
        size = value.shape[1] // 2
        value = value[:, :size] + value[:, size:]
        first, second = value[:, : size // 2], value[:, size // 2 :]

        @pl.when(pl.program_id(0) == 0)
        def _():
            kept_ref[...] = jnp.zeros_like(kept_ref)
            sent_ref[...] = jnp.zeros_like(sent_ref)

        kept_ref[...] += jnp.where(odd, second, first)
        sent_ref[...] += jnp.where(odd, first, second)


def sweep_step(parity, volume, ratios, columns, weights, weights_turned, tiles, camera, following):
    exposures, count, depth = volume.shape
    pixels = weights.shape[2]
    block = count // STEPS
    back, forward = camera is not None, following is not None
    rows, tile_values, members = columns

    def fixed(shape, place):
        return pl.BlockSpec(shape, lambda i: place)

    def column_spec(index):
        return pl.BlockSpec((1, block, LANES), lambda i: (index, i, 0))

    volume_spec = pl.BlockSpec((exposures, block, depth), lambda i: (0, i, 0))
    operands = [parity, volume]
    specs = [pl.BlockSpec(memory_space=pltpu.SMEM), volume_spec]
    shapes, outs = [], []
    if back:
        operands += [*ratios, tile_values, members, weights]
        specs += [fixed((tiles, pixels), (0, 0))] * 2
        specs += [column_spec(camera)] * 2
        specs.append(fixed((1,) + weights.shape[1:], (camera, 0, 0, 0)))
        shapes.append(jax.ShapeDtypeStruct(volume.shape, jnp.float32))
        outs.append(volume_spec)
    if forward:
        operands += [rows, members, weights_turned]
        specs += [
            pl.BlockSpec((1, 1, block), lambda i: (following, 0, i)),
            column_spec(following),
            fixed((1,) + weights_turned.shape[1:], (following, 0, 0, 0)),
        ]
        shapes += [jax.ShapeDtypeStruct((tiles, pixels), jnp.float32)] * 2
        outs += [fixed((tiles, pixels), (0, 0))] * 2
    if not forward:
        shape = (exposures, count + SPARE, depth)
        shapes.append(jax.ShapeDtypeStruct(shape, jnp.int16))
        outs.append(fixed(shape, (0, 0, 0)))
    result = pl.pallas_call(
        functools.partial(sweep_body, back, forward),
        grid=(STEPS,),
        in_specs=specs,
        out_specs=outs,
        out_shape=shapes,
        name="sweep",
    )(*operands)
    return (result[0] if back else volume), (result[-2:] if forward else result[-1])


def column_tables(target, member):
    shape = target.shape + (LANES,)
    tile_values = jnp.broadcast_to(target.astype(jnp.bfloat16)[..., None], shape)
    members = jnp.broadcast_to(member.astype(jnp.bfloat16)[..., None], shape)
    return target[:, None, :], tile_values, members


def partner_of(count, bit):
    return [(i, i ^ bit) for i in range(count)]


def shared_ratio(kept, sent, picture):
    count = lax.axis_size("wide")
    pair = partner_of(count, 1)
    total = kept + lax.ppermute(sent, "wide", pair)
    bit = 2
    while bit < count:
        total = total + lax.ppermute(total, "wide", partner_of(count, bit))
        bit *= 2
    ratio = (picture - jnp.log(total + 1.0)).astype(jnp.bfloat16)
    return ratio, lax.ppermute(ratio, "wide", pair)


def reconstructed(initial, images, blocks, lib_index, tile_map):
    count = lax.axis_size("wide")
    own_index = lax.axis_index("wide")
    exposures, brick_x, brick_y, depth = initial.shape
    cameras, tile_rows, tile_cols, pixels = images.shape[1:]
    tile_count = tile_rows * tile_cols
    tiles = count * tile_count
    columns = brick_x * brick_y
    strip = own_index - count // 2 + tile_map // tile_count
    target = strip * tile_count + tile_map % tile_count
    missing = -(-tiles // LANES) * LANES
    target = jnp.where((strip >= 0) & (strip < count), target, missing)
    tables = column_tables(
        target.reshape(cameras, columns), lib_index.reshape(cameras, columns)
    )
    parity = (own_index % 2).reshape(1)
    pictures = jnp.log(images.reshape(exposures, cameras, tile_count, pixels) + 1.0)
    by_core = jnp.broadcast_to(pictures[None], (count // 2,) + pictures.shape)
    by_core = by_core.reshape((count, cameras, tile_count, pixels))
    gathered = lax.all_to_all(by_core, "wide", split_axis=0, concat_axis=0, tiled=True)
    gathered = gathered.transpose(1, 0, 2, 3).reshape(cameras, tiles, pixels)
    turned = blocks.transpose(0, 1, 3, 2)
    volume = initial.reshape(exposures, columns, depth)
    order = [camera for _ in range(SWEEPS) for camera in range(cameras)]
    step = functools.partial(
        sweep_step, columns=tables, weights=blocks, weights_turned=turned, tiles=tiles
    )
    volume, partial_value = step(parity, volume, None, camera=None, following=order[0])
    for place, camera in enumerate(order):
        following = order[place + 1] if place + 1 < len(order) else None
        ratios = shared_ratio(*partial_value, gathered[camera])
        volume, partial_value = step(parity, volume, ratios, camera=camera, following=following)
    return volume, partial_value


def neighbours(own):
    def shifted(value, axis, step):
        count = lax.axis_size(axis)
        pairs = [(i, i + step) for i in range(count) if 0 <= i + step < count]
        return lax.ppermute(value, axis, pairs)

    near, far = shifted(own, "narrow", 1), shifted(own, "narrow", -1)
    left, right = shifted(own, "wide", 1), shifted(own, "wide", -1)
    left_pair = shifted(jnp.stack([near, far]), "wide", 1)
    right_near, right_far = shifted(right, "narrow", 1), shifted(right, "narrow", -1)
    return [left, right, near, far, left_pair, right_near, right_far]


def body(initial, images, blocks, lib_index, tile_map, win_x, win_y, win_z):
    volume, code = reconstructed(initial, images, blocks, lib_index, tile_map)
    starts = jnp.stack([win_x.reshape(-1), win_y.reshape(-1), win_z.reshape(-1)], axis=1)
    correlation = window_correlations(volume, neighbours(code), starts)
    return (volume.reshape(initial.shape), correlation.reshape(1, 1, starts.shape[0], DISP * DISP * DISP))


def solution(mesh):
    placed = (
        P(None, "wide", "narrow", None),
        P(None, None, "wide", "narrow", None),
        P(),
        P(None, "wide", "narrow"),
        P(None, "wide", "narrow"),
        P("wide", "narrow", None),
        P("wide", "narrow", None),
        P("wide", "narrow", None),
    )
    return jax.shard_map(
        body,
        mesh=mesh,
        in_specs=placed,
        out_specs=(P(None, "wide", "narrow", None), P("wide", "narrow", None, None)),
        check_vma=False,
    )
```

```python
import functools
import numpy as np
import jax
import jax.numpy as jnp
from jax import lax
from jax.experimental import pallas as pl
from jax.experimental.pallas import tpu as pltpu
from jax.sharding import PartitionSpec as P

WIN = 64
DISP = 16
SWEEPS = 2
TERMS = 4
LEVELS = 65535.0
MIDDLE = 32768.0
GRAIN = 16.0
SPARE = 16
STEPS = 1
UNROLL = False
LIMIT = 24 * 1024 * 1024
FOLD = 16
GROUPS = 2
THIRD = 1
SPLIT = 4


def split_table(table):
    high = np.asarray(table, np.float32).astype(jnp.bfloat16)
    low = (np.asarray(table, np.float64) - high.astype(np.float64)).astype(np.float32)
    return high, low.astype(jnp.bfloat16)


def window_tables(count):
    half = WIN // 2 + 1
    unit = 2.0 * np.pi / WIN
    index = np.arange(WIN)
    shifts = np.arange(DISP) - DISP // 2
    turn = unit * np.outer(index, index)
    cos_full, sin_full = np.cos(turn), np.sin(turn)
    rows_y = -(-2 * half // 8) * 8
    first = np.zeros((rows_y, WIN))
    first[0 : 2 * half : 2] = cos_full[:half]
    first[1 : 2 * half : 2] = -sin_full[:half]
    high, low = split_table(first)
    table_y = np.concatenate([high, high, low], axis=1)
    second = np.block([[cos_full, sin_full], [-sin_full, cos_full]])
    high, low = split_table(second)
    table_x = np.concatenate([high, high, low], axis=1)
    third = np.zeros((2, 2, WIN, 2, 2, WIN))
    for e in range(2):
        third[0, e, :, e, 0] = cos_full
        third[1, e, :, e, 0] = sin_full
        third[0, e, :, e, 1] = -sin_full
        third[1, e, :, e, 1] = cos_full
    high, low = split_table(third.reshape(4 * WIN, 4 * WIN))
    table_z = np.concatenate([high, high, low], axis=0)
    part = unit * np.outer(index, shifts)
    cos_part, sin_part = np.cos(part), np.sin(part)
    fourth = np.zeros((4, WIN, 2 * WIN))
    fourth[..., :DISP] = np.stack([cos_part, cos_part, -sin_part, sin_part])
    fourth[..., DISP : 2 * DISP] = np.stack([sin_part, sin_part, cos_part, -cos_part])
    fourth = fourth.reshape(4 * WIN, 2 * WIN)
    shifted = np.stack([np.roll(fourth, w * 2 * DISP, axis=1) for w in range(count)])
    high, low = split_table(shifted)
    table_iz = np.concatenate([high, high, low], axis=1)
    high, low = split_table(np.concatenate([cos_part.T, sin_part.T], axis=1))
    table_ix = np.concatenate([high, high, low], axis=1)
    weight = np.full(half, 2.0)
    weight[0] = weight[-1] = 1.0
    pad = -(-half // 16) * 16
    last = np.zeros((2 * DISP, pad))
    last[:DISP, :half] = cos_part.T[:, :half] * weight
    last[DISP:, :half] = sin_part.T[:, :half] * weight
    high, low = split_table(last)
    table_iy = np.concatenate([high, high, low], axis=1)
    return table_y, table_x, table_z, table_iz, table_ix, table_iy


def halves(value):
    high = value.astype(jnp.bfloat16)
    low = (value - high.astype(jnp.float32)).astype(jnp.bfloat16)
    return high, low


def stacked(value):
    high, low = halves(value)
    return jnp.concatenate([high, low, high], axis=0)


def mul(left, right):
    return jnp.dot(left, right, preferred_element_type=jnp.float32)


def window_body(count, starts, *refs):
    own, left, right, near, far, left_pair, right_near, right_far = refs[:8]
    t_y, t_x, t_z, t_iz, t_ix, t_iy, out = refs[8:15]
    ext, levels, sems, folded, spectrum, high_ref, low_ref, product, turned = refs[15:]
    half_win = WIN // 2
    half = WIN // 2 + 1
    rows_y = t_y.shape[0]
    pad = t_iy.shape[1] // 3
    sources = [left_pair.at[0], left, left_pair.at[1], near, far, right_near, right, right_far]
    copies = [
        pltpu.make_async_copy(source, levels.at[i], sems.at[i])
        for i, source in enumerate(sources)
    ]
    copies.append(pltpu.make_async_copy(own, ext.at[len(sources) // 2], sems.at[len(sources)]))
    for copy in copies:
        copy.start()
    product[...] = jnp.zeros_like(product)
    turned[...] = jnp.zeros_like(turned)
    for copy in copies:
        copy.wait()
    exposures, columns = ext.shape[1:3]

    def decode(i, done):
        brick = jnp.where(i < len(sources) // 2, i, i + 1)
        for e in range(exposures):
            scale = levels[i, e, columns:, :].astype(jnp.int32).astype(jnp.float32)
            least, width = scale[:1] / GRAIN, scale[1:2]
            step = width / (GRAIN * LEVELS)
            base = least + MIDDLE * step
            present = jnp.where(width > 0.0, 1.0, 0.0)
            for start in range(0, columns, columns // 4):
                place = slice(start, start + columns // 4)
                level = levels[i, e, place, :].astype(jnp.int32).astype(jnp.float32)
                ext[brick, e, place, :] = jnp.exp(level * step + base) * present
        return done

    lax.fori_loop(0, len(sources), decode, 0)
    lane = lax.broadcasted_iota(jnp.int32, (WIN, 2 * WIN), 1)
    row = lax.broadcasted_iota(jnp.int32, (half_win, 2 * WIN), 0)
    left_lane = lane < WIN
    left_row = left_lane[:1]

    def one_window(w, carry):
        sx, sy, sz = starts[w, 0], starts[w, 1], starts[w, 2]
        keep = (left_lane & (lane >= sz)) | (~left_lane & (lane < sz + WIN))
        below = row >= sy

        def fold(i, total):
            for j in range(FOLD):
                x = i * FOLD + j
                brick = jnp.where(x >= half_win, 3, jnp.where(x >= sx, 0, 6))
                inner = pl.ds(pl.multiple_of((x & (half_win - 1)) * half_win, half_win), half_win)
                values = []
                for e in range(2):
                    low = ext[brick + 0, e, inner]
                    same = ext[brick + 1, e, inner]
                    high = ext[brick + 2, e, inner]
                    values.append(jnp.concatenate([jnp.where(below, low, high), same], axis=0))
                stay = jnp.where(left_lane, values[0], values[1])
                move = jnp.where(left_lane, values[1], values[0])
                value = jnp.where(keep, stay, pltpu.roll(move, WIN, 1))
                folded[x] = value
                total = total + value
            return total

        total = lax.fori_loop(0, WIN // FOLD, fold, jnp.zeros((WIN, 2 * WIN), jnp.float32))
        total = jnp.sum(total, axis=0, keepdims=True)
        scale = 1.0 / WIN**3
        mean = jnp.where(
            left_row,
            jnp.sum(jnp.where(left_row, total, 0.0), axis=1, keepdims=True) * scale,
            jnp.sum(jnp.where(left_row, 0.0, total), axis=1, keepdims=True) * scale,
        )

        def first(i, square):
            for g in range(GROUPS):
                start = (i * GROUPS + g) * 8
                results = []
                for j in range(0, 8, 2):
                    values = [folded[start + j + k] - mean for k in range(2)]
                    for value in values:
                        square = square + value * value
                    result = mul(t_y[...], stacked(jnp.concatenate(values, axis=1)))
                    results += [result[:, : 2 * WIN], result[:, 2 * WIN :]]
                spectrum[:, pl.ds(pl.multiple_of(start, 8), 8), :] = jnp.swapaxes(
                    jnp.stack(results), 0, 1
                )
            return square

        square = lax.fori_loop(0, WIN // (8 * GROUPS), first, jnp.zeros((WIN, 2 * WIN), jnp.float32))
        square = jnp.sum(square, axis=0, keepdims=True)
        power_0 = jnp.sum(jnp.where(left_row, square, 0.0), axis=1, keepdims=True) * scale
        power_1 = jnp.sum(jnp.where(left_row, 0.0, square), axis=1, keepdims=True) * scale
        norm = jnp.sqrt(power_0 + 1e-06) * jnp.sqrt(power_1 + 1e-06)
        factor = 1.0 / (WIN**3 * WIN**1.5) / norm

        def second(i, done):
            for j in range(0, 11, 2):
                width = min(2, 11 - j)
                k = i * 11 + j
                values = [
                    spectrum[pl.ds(2 * (k + n), 2)].reshape(2 * WIN, 2 * WIN) for n in range(width)
                ]
                result = mul(t_x[...], stacked(jnp.concatenate(values, axis=1)))
                for n in range(width):
                    part = result[:, 2 * WIN * n : 2 * WIN * (n + 1)]
                    part = jnp.concatenate([part[:WIN], part[WIN:]], axis=1)
                    place = pl.ds(pl.multiple_of((k + n) * WIN, WIN), WIN)
                    high_ref[place, :], low_ref[place, :] = halves(part)
            return done

        lax.fori_loop(0, half // 11, second, 0)
        block = half * WIN // (THIRD * SPLIT)

        def third(i, done):
            for g in range(SPLIT):
                place = pl.ds(pl.multiple_of((i * SPLIT + g) * block, block), block)
                high, low = high_ref[place, :], low_ref[place, :]
                value = mul(jnp.concatenate([high, low, high], axis=1), t_z[...])
                one, two = value[:, : 2 * WIN] * factor, value[:, 2 * WIN :]
                cross = jnp.concatenate([one * two, one * pltpu.roll(two, WIN, 1)], axis=1)
                high, low = halves(cross)
                product[place, :] += mul(jnp.concatenate([high, low, high], axis=1), t_iz[w])
            return done

        lax.fori_loop(0, THIRD, third, 0)
        return carry

    lax.fori_loop(0, count, one_window, 0)

    real_lane = lane % (2 * DISP) < DISP

    def fifth(i, done):
        for j in range(11):
            k = i * 11 + j
            value = product[pl.ds(pl.multiple_of(k * WIN, WIN), WIN), :]
            turn = jnp.where(
                real_lane, -pltpu.roll(value, 2 * WIN - DISP, 1), pltpu.roll(value, DISP, 1)
            )
            value = jnp.concatenate([value, turn], axis=0)
            turned[pl.ds(k, DISP, stride=pad), :] = mul(t_ix[...], stacked(value))
        return done

    lax.fori_loop(0, half // 11, fifth, 0)
    for d in range(DISP):
        value = mul(t_iy[...], stacked(turned[d * pad : (d + 1) * pad, :]))
        out[:, d * 2 * WIN : (d + 1) * 2 * WIN] = value[:DISP] - pltpu.roll(
            value[DISP:], 2 * WIN - DISP, 1
        )


def window_correlations(own, bricks, starts):
    count = starts.shape[0]
    tables = window_tables(count)
    half = WIN // 2 + 1
    rows_y = tables[0].shape[0]
    pad = tables[5].shape[1] // 3
    spread = bricks[0].shape
    vmem = pl.BlockSpec(memory_space=pltpu.VMEM)
    result = pl.pallas_call(
        functools.partial(window_body, count),
        out_shape=jax.ShapeDtypeStruct((DISP, DISP * 2 * WIN), jnp.float32),
        in_specs=[pl.BlockSpec(memory_space=pltpu.SMEM)]
        + [pl.BlockSpec(memory_space=pl.ANY)] * 8
        + [vmem] * 6,
        out_specs=vmem,
        scratch_shapes=[
            pltpu.VMEM((9,) + own.shape, jnp.float32),
            pltpu.VMEM((8,) + spread, jnp.int16),
            pltpu.SemaphoreType.DMA((9,)),
            pltpu.VMEM((WIN, WIN, 2 * WIN), jnp.float32),
            pltpu.VMEM((rows_y, WIN, 2 * WIN), jnp.float32),
            pltpu.VMEM((half * WIN, 4 * WIN), jnp.bfloat16),
            pltpu.VMEM((half * WIN, 4 * WIN), jnp.bfloat16),
            pltpu.VMEM((half * WIN, 2 * WIN), jnp.float32),
            pltpu.VMEM((DISP * pad, 2 * WIN), jnp.float32),
        ],
        name="windows",
    )(starts, own, *bricks, *[jnp.asarray(t) for t in tables])
    result = result.reshape(DISP, DISP, 2 * WIN // (2 * DISP), 2 * DISP)[:, :, :count, :DISP]
    return result.transpose(2, 1, 0, 3).reshape(count, DISP**3)


LANES = 128


def chosen_products(value, member, weights_ref):
    count = weights_ref.shape[1]
    half_count = count // 2
    size = weights_ref.shape[2]
    copies = value.shape[0] // member.shape[0]
    total = None
    for start in range(0, half_count, TERMS):
        picked, tables = [], []
        for j in range(start, min(start + TERMS, half_count)):
            hit = (member == j) | (member == j + half_count)
            hit = jnp.concatenate([hit] * copies, axis=0)
            picked.append(jnp.where(hit, value, jnp.zeros_like(value)))
            tables.append(
                jnp.concatenate([weights_ref[0, j], weights_ref[0, j + half_count]], axis=1)
            )
        term = mul(jnp.concatenate(picked, axis=1), jnp.concatenate(tables, axis=0))
        total = term if total is None else total + term
    upper = jnp.concatenate([member.astype(jnp.float32)] * copies, axis=0) >= half_count
    return jnp.where(upper, total[:, size:], total[:, :size])


def placed_tiles(tile, count):
    columns = lax.broadcasted_iota(jnp.int32, tile.shape, 1).astype(jnp.float32)
    columns = columns.astype(tile.dtype)
    one, zero = jnp.ones_like(tile), jnp.zeros_like(tile)
    parts = [
        jnp.where(tile - start == columns, one, zero) for start in range(0, count, LANES)
    ]
    return jnp.concatenate(parts, axis=1)[:, :count]


def sweep_body(back, forward, parity_ref, *refs):
    refs = list(refs)
    volume_ref = refs.pop(0)
    if back:
        own_ratio, other_ratio, back_tile, back_member, back_weights = refs[:5]
        refs = refs[5:]
    if forward:
        next_row, next_member, next_weights = refs[:3]
        refs = refs[3:]
    if back:
        volume_out = refs.pop(0)
    exposures, columns, depth = volume_ref.shape
    block = columns // STEPS
    odd = parity_ref[0] == 1
    if back:
        own, other = own_ratio[...], other_ratio[...]
        ratios = [jnp.where(odd, other, own), jnp.where(odd, own, other)]
        ratios = jnp.concatenate(ratios, axis=1)
    tiles = refs[0].shape[0]

    def one_block(i, total):
        place = pl.ds(pl.multiple_of(i * block, block), block)
        volume = volume_ref[:, place, :].reshape(exposures * block, depth)
        if back:
            placement = placed_tiles(back_tile[0, place, :], own.shape[0])
            spread = mul(placement, ratios).astype(jnp.bfloat16)
            spread = jnp.concatenate(
                [spread[:, e * LANES : (e + 1) * LANES] for e in range(exposures)], axis=0
            )
            member = back_member[0, place, :]
            volume = volume * jnp.exp(chosen_products(spread, member, back_weights))
            volume_out[:, place, :] = volume.reshape(exposures, block, depth)
        if forward:
            member = next_member[0, place, :]
            projected = chosen_products(volume.astype(jnp.bfloat16), member, next_weights)
            parts = list(halves(projected))
            parts = [p[e * block : (e + 1) * block] for p in parts for e in range(exposures)]
            rows = lax.broadcasted_iota(jnp.int32, (tiles, block), 0)
            hit = next_row[0, pl.ds(i, 1), :] == rows
            placement = jnp.where(hit, 1.0, 0.0).astype(jnp.bfloat16)
            value = mul(placement, jnp.concatenate(parts, axis=1))
            size = value.shape[1] // 2
            total = total + (value[:, :size] + value[:, size:])
        return total

    if forward:
        start = jnp.zeros((tiles, exposures * depth), jnp.float32)
        if UNROLL:
            for i in range(STEPS):
                start = one_block(i, start)
            total = start
        else:
            total = lax.fori_loop(0, STEPS, one_block, start)
        kept_ref, sent_ref = refs
        first, second = total[:, :depth], total[:, depth:]
        kept_ref[...] = jnp.where(odd, second, first)
        sent_ref[...] = jnp.where(odd, first, second)
    else:
        lax.fori_loop(0, STEPS, one_block, 0)
        (code_ref,) = refs
        for e in range(exposures):
            logs = jnp.log(jnp.maximum(volume_out[e], 1e-37))
            least = jnp.floor(jnp.min(logs, axis=0, keepdims=True) * GRAIN)
            width = jnp.floor(jnp.max(logs, axis=0, keepdims=True) * GRAIN - least) + 1.0
            rate = (GRAIN * LEVELS) / width
            level = jnp.floor((logs - least / GRAIN) * rate + 0.5) - MIDDLE
            code_ref[e, :columns, :] = level.astype(jnp.int32).astype(jnp.int16)
            row = lax.broadcasted_iota(jnp.int32, (SPARE, depth), 0)
            extra = jnp.where(row == 0, least, jnp.where(row == 1, width, 0.0))
            code_ref[e, columns:, :] = extra.astype(jnp.int32).astype(jnp.int16)


def sweep_step(parity, volume, ratios, columns, weights, weights_turned, tiles, camera, following):
    exposures, count, depth = volume.shape
    pixels = weights.shape[2]
    back, forward = camera is not None, following is not None
    rows, tile_values, members = columns

    def taken(value, index):
        shape = (1,) + value.shape[1:]
        return pl.BlockSpec(shape, lambda i: (index,) + (0,) * (len(shape) - 1))

    def whole(shape):
        return pl.BlockSpec(shape, lambda i: (0,) * len(shape))

    operands = [parity, volume]
    specs = [pl.BlockSpec(memory_space=pltpu.SMEM), whole(volume.shape)]
    shapes = []
    if back:
        operands += [*ratios, tile_values, members, weights]
        specs += [whole((tiles, pixels))] * 2
        specs += [taken(tile_values, camera), taken(members, camera), taken(weights, camera)]
        shapes.append(jax.ShapeDtypeStruct(volume.shape, jnp.float32))
    if forward:
        operands += [rows, members, weights_turned]
        specs += [taken(value, following) for value in operands[-3:]]
        shapes += [jax.ShapeDtypeStruct((tiles, pixels), jnp.float32)] * 2
    else:
        shapes.append(jax.ShapeDtypeStruct((exposures, count + SPARE, depth), jnp.int16))
    result = pl.pallas_call(
        functools.partial(sweep_body, back, forward),
        grid=(1,),
        in_specs=specs,
        out_specs=[whole(value.shape) for value in shapes],
        out_shape=shapes,
        compiler_params=pltpu.CompilerParams(vmem_limit_bytes=LIMIT),
        name="sweep",
    )(*operands)
    return (result[0] if back else volume), (result[-2:] if forward else result[-1])


def column_tables(target, member):
    shape = target.shape + (LANES,)
    tile_values = jnp.broadcast_to(target.astype(jnp.bfloat16)[..., None], shape)
    members = jnp.broadcast_to(member.astype(jnp.bfloat16)[..., None], shape)
    rows = target.reshape(target.shape[0], STEPS, target.shape[1] // STEPS)
    return rows, tile_values, members


def partner_of(count, bit):
    return [(i, i ^ bit) for i in range(count)]


def shared_ratio(kept, sent, picture):
    count = lax.axis_size("wide")
    pair = partner_of(count, 1)
    total = kept + lax.ppermute(sent, "wide", pair)
    bit = 2
    while bit < count:
        total = total + lax.ppermute(total, "wide", partner_of(count, bit))
        bit *= 2
    ratio = (picture - jnp.log(total + 1.0)).astype(jnp.bfloat16)
    return ratio, lax.ppermute(ratio, "wide", pair)


def reconstructed(initial, images, blocks, lib_index, tile_map):
    count = lax.axis_size("wide")
    own_index = lax.axis_index("wide")
    exposures, brick_x, brick_y, depth = initial.shape
    cameras, tile_rows, tile_cols, pixels = images.shape[1:]
    tile_count = tile_rows * tile_cols
    tiles = count * tile_count
    columns = brick_x * brick_y
    strip = own_index - count // 2 + tile_map // tile_count
    target = strip * tile_count + tile_map % tile_count
    missing = -(-tiles // LANES) * LANES
    target = jnp.where((strip >= 0) & (strip < count), target, missing)
    tables = column_tables(
        target.reshape(cameras, columns), lib_index.reshape(cameras, columns)
    )
    parity = (own_index % 2).reshape(1)
    pictures = jnp.log(images.reshape(exposures, cameras, tile_count, pixels) + 1.0)
    by_core = jnp.broadcast_to(pictures[None], (count // 2,) + pictures.shape)
    by_core = by_core.reshape((count, cameras, tile_count, pixels))
    gathered = lax.all_to_all(by_core, "wide", split_axis=0, concat_axis=0, tiled=True)
    gathered = gathered.transpose(1, 0, 2, 3).reshape(cameras, tiles, pixels)
    turned = blocks.transpose(0, 1, 3, 2)
    volume = initial.reshape(exposures, columns, depth)
    order = [camera for _ in range(SWEEPS) for camera in range(cameras)]
    step = functools.partial(
        sweep_step, columns=tables, weights=blocks, weights_turned=turned, tiles=tiles
    )
    volume, partial_value = step(parity, volume, None, camera=None, following=order[0])
    for place, camera in enumerate(order):
        following = order[place + 1] if place + 1 < len(order) else None
        ratios = shared_ratio(*partial_value, gathered[camera])
        volume, partial_value = step(parity, volume, ratios, camera=camera, following=following)
    return volume, partial_value


def neighbours(own):
    def shifted(value, axis, step):
        count = lax.axis_size(axis)
        pairs = [(i, i + step) for i in range(count) if 0 <= i + step < count]
        return lax.ppermute(value, axis, pairs)

    near, far = shifted(own, "narrow", 1), shifted(own, "narrow", -1)
    left, right = shifted(own, "wide", 1), shifted(own, "wide", -1)
    near, far, left, right = lax.optimization_barrier((near, far, left, right))
    left_pair = shifted(jnp.stack([near, far]), "wide", 1)
    right_near, right_far = shifted(right, "narrow", 1), shifted(right, "narrow", -1)
    return [left, right, near, far, left_pair, right_near, right_far]


def body(initial, images, blocks, lib_index, tile_map, win_x, win_y, win_z):
    volume, code = reconstructed(initial, images, blocks, lib_index, tile_map)
    starts = jnp.stack([win_x.reshape(-1), win_y.reshape(-1), win_z.reshape(-1)], axis=1)
    correlation = window_correlations(volume, neighbours(code), starts)
    return (volume.reshape(initial.shape), correlation.reshape(1, 1, starts.shape[0], DISP * DISP * DISP))


def solution(mesh):
    placed = (
        P(None, "wide", "narrow", None),
        P(None, None, "wide", "narrow", None),
        P(),
        P(None, "wide", "narrow"),
        P(None, "wide", "narrow"),
        P("wide", "narrow", None),
        P("wide", "narrow", None),
        P("wide", "narrow", None),
    )
    return jax.shard_map(
        body,
        mesh=mesh,
        in_specs=placed,
        out_specs=(P(None, "wide", "narrow", None), P("wide", "narrow", None, None)),
        check_vma=False,
    )
```

```python
import functools
import numpy as np
import jax
import jax.numpy as jnp
from jax import lax
from jax.experimental import pallas as pl
from jax.experimental.pallas import tpu as pltpu
from jax.sharding import PartitionSpec as P

WIN = 64
DISP = 16
SWEEPS = 2
TERMS = 4
LEVELS = 65535.0
MIDDLE = 32768.0
GRAIN = 16.0
SPARE = 16
STEPS = 1
UNROLL = False
LIMIT = 24 * 1024 * 1024
WIDE_LIMIT = 32 * 1024 * 1024
GROUPS = 2
THIRD = 1
SPLIT = 4


def split_table(table):
    high = np.asarray(table, np.float32).astype(jnp.bfloat16)
    low = (np.asarray(table, np.float64) - high.astype(np.float64)).astype(np.float32)
    return high, low.astype(jnp.bfloat16)


def window_tables(count):
    half = WIN // 2 + 1
    unit = 2.0 * np.pi / WIN
    index = np.arange(WIN)
    shifts = np.arange(DISP) - DISP // 2
    turn = unit * np.outer(index, index)
    cos_full, sin_full = np.cos(turn), np.sin(turn)
    rows_y = -(-2 * half // 8) * 8
    first = np.zeros((rows_y, WIN))
    first[0 : 2 * half : 2] = cos_full[:half]
    first[1 : 2 * half : 2] = -sin_full[:half]
    high, low = split_table(first)
    table_y = np.concatenate([high, high, low], axis=1)
    second = np.block([[cos_full, sin_full], [-sin_full, cos_full]])
    high, low = split_table(second)
    table_x = np.concatenate([high, high, low], axis=1)
    third = np.zeros((2, 2, WIN, 2, 2, WIN))
    for e in range(2):
        third[0, e, :, e, 0] = cos_full
        third[1, e, :, e, 0] = sin_full
        third[0, e, :, e, 1] = -sin_full
        third[1, e, :, e, 1] = cos_full
    high, low = split_table(third.reshape(4 * WIN, 4 * WIN))
    table_z = np.concatenate([high, high, low], axis=0)
    part = unit * np.outer(index, shifts)
    cos_part, sin_part = np.cos(part), np.sin(part)
    fourth = np.zeros((4, WIN, 2 * WIN))
    fourth[..., :DISP] = np.stack([cos_part, cos_part, -sin_part, sin_part])
    fourth[..., DISP : 2 * DISP] = np.stack([sin_part, sin_part, cos_part, -cos_part])
    fourth = fourth.reshape(4 * WIN, 2 * WIN)
    shifted = np.stack([np.roll(fourth, w * 2 * DISP, axis=1) for w in range(count)])
    high, low = split_table(shifted)
    table_iz = np.concatenate([high, high, low], axis=1)
    high, low = split_table(np.concatenate([cos_part.T, sin_part.T], axis=1))
    table_ix = np.concatenate([high, high, low], axis=1)
    weight = np.full(half, 2.0)
    weight[0] = weight[-1] = 1.0
    pad = -(-half // 16) * 16
    last = np.zeros((2 * DISP, pad))
    last[:DISP, :half] = cos_part.T[:, :half] * weight
    last[DISP:, :half] = sin_part.T[:, :half] * weight
    high, low = split_table(last)
    table_iy = np.concatenate([high, high, low], axis=1)
    return table_y, table_x, table_z, table_iz, table_ix, table_iy


def halves(value):
    high = value.astype(jnp.bfloat16)
    low = (value - high.astype(jnp.float32)).astype(jnp.bfloat16)
    return high, low


def stacked(value):
    high, low = halves(value)
    return jnp.concatenate([high, low, high], axis=0)


def mul(left, right):
    return jnp.dot(left, right, preferred_element_type=jnp.float32)


def decode(level_ref, target_ref):
    exposures, columns = target_ref.shape[:2]
    for e in range(exposures):
        scale = level_ref[e, columns:, :].astype(jnp.int32).astype(jnp.float32)
        least, width = scale[:1] / GRAIN, scale[1:2]
        step = width / (GRAIN * LEVELS)
        base = least + MIDDLE * step
        present = jnp.where(width > 0.0, 1.0, 0.0)
        for start in range(0, columns, columns // 4):
            place = slice(start, start + columns // 4)
            level = level_ref[e, place, :].astype(jnp.int32).astype(jnp.float32)
            target_ref[e, place, :] = jnp.exp(level * step + base) * present


def first_stage(ext, brick_of, start, mean, table, spectrum_ref):
    half_win = WIN // 2
    _, sy, sz = start
    lane = lax.broadcasted_iota(jnp.int32, (WIN, 2 * WIN), 1)
    row = lax.broadcasted_iota(jnp.int32, (half_win, 2 * WIN), 0)
    left_lane = lane < WIN
    keep = (left_lane & (lane >= sz)) | (~left_lane & (lane < sz + WIN))
    below = row >= sy

    def fold(x):
        brick = brick_of(x)
        inner = pl.ds(pl.multiple_of(x * half_win, half_win), half_win)
        values = []
        for e in range(2):
            low, high = ext[brick, e, inner], ext[brick + 2, e, inner]
            same = ext[brick + 1, e, inner]
            values.append(jnp.concatenate([jnp.where(below, low, high), same], axis=0))
        stay = jnp.where(left_lane, values[0], values[1])
        move = jnp.where(left_lane, values[1], values[0])
        return jnp.where(keep, stay, pltpu.roll(move, WIN, 1)) - mean

    def one_group(i, sums):
        total, square = sums
        for g in range(GROUPS):
            begin = (i * GROUPS + g) * 8
            results = []
            for j in range(0, 8, 2):
                values = [fold(begin + j + k) for k in range(2)]
                for value in values:
                    total = total + value
                    square = square + value * value
                result = mul(table, stacked(jnp.concatenate(values, axis=1)))
                results += [result[:, : 2 * WIN], result[:, 2 * WIN :]]
            spectrum_ref[:, pl.ds(pl.multiple_of(begin, 8), 8), :] = jnp.swapaxes(
                jnp.stack(results), 0, 1
            )
        return total, square

    zero = jnp.zeros((WIN, 2 * WIN), jnp.float32)
    total, square = lax.fori_loop(0, half_win // (8 * GROUPS), one_group, (zero, zero))
    return [jnp.sum(value, axis=0, keepdims=True) for value in (total, square)]


def by_exposure(value):
    left = lax.broadcasted_iota(jnp.int32, value.shape, 1) < WIN
    return (
        jnp.sum(jnp.where(left, value, 0.0), axis=1, keepdims=True),
        jnp.sum(jnp.where(left, 0.0, value), axis=1, keepdims=True),
    )


def middle_body(count, starts, own, near, far, t_y, spectrum_out, stats_out, ext, levels, sems):
    copies = [
        pltpu.make_async_copy(source, target, sems.at[i])
        for i, (source, target) in enumerate(
            [(own, ext.at[1]), (near, levels.at[0]), (far, levels.at[1])]
        )
    ]
    for copy in copies:
        copy.start()
    for copy in copies:
        copy.wait()
    decode(levels.at[0], ext.at[0])
    decode(levels.at[1], ext.at[2])
    exposures, columns, depth = ext.shape[1:]
    sums = [jnp.sum(ext[1, e], axis=0, keepdims=True) for e in range(exposures)]
    lane = lax.broadcasted_iota(jnp.int32, (1, depth), 1)

    def one_window(w, done):
        start = [starts[w, n] for n in range(3)]
        inside = (lane >= start[2]) & (lane < start[2] + WIN)
        means = [
            jnp.sum(jnp.where(inside, value, 0.0), axis=1, keepdims=True) / (columns * WIN)
            for value in sums
        ]
        mean = jnp.where(lane < WIN, means[0], means[1])
        total, square = first_stage(
            ext, lambda x: 0, start, mean, t_y[...], spectrum_out.at[w]
        )
        spare = jnp.zeros((5, depth), jnp.float32)
        stats_out[w] = jnp.concatenate([mean, total, square, spare], axis=0)
        return done

    lax.fori_loop(0, count, one_window, 0)


def window_body(count, starts, stats, *refs):
    middle, left, right, left_near, left_far, right_near, right_far = refs[:7]
    t_y, t_x, t_z, t_iz, t_ix, t_iy, out = refs[7:14]
    ext, levels, sems, spectrum, high_ref, low_ref, product, turned = refs[14:]
    half = WIN // 2 + 1
    pad = t_iy.shape[1] // 3
    sources = [left_near, left, left_far, right_near, right, right_far]
    copies = [
        pltpu.make_async_copy(source, levels.at[i], sems.at[i])
        for i, source in enumerate(sources)
    ]

    def middle_copy(w):
        target = spectrum.at[:, pl.ds(WIN // 2, WIN // 2), :]
        return pltpu.make_async_copy(middle.at[w], target, sems.at[len(sources)])

    middle_copy(0).start()
    for copy in copies:
        copy.start()
    product[...] = jnp.zeros_like(product)
    turned[...] = jnp.zeros_like(turned)
    for copy in copies:
        copy.wait()

    def decode_one(i, done):
        decode(levels.at[i], ext.at[i])
        return done

    lax.fori_loop(0, len(sources), decode_one, 0)
    lane = lax.broadcasted_iota(jnp.int32, (WIN, 2 * WIN), 1)

    def one_window(w, carry):
        start = [starts[w, n] for n in range(3)]
        known = stats[w]
        total, square = first_stage(
            ext,
            lambda x: jnp.where(x >= start[0], 0, 3),
            start,
            known[:1],
            t_y[...],
            spectrum,
        )
        scale = 1.0 / WIN**3
        totals, squares = by_exposure(total + known[1:2]), by_exposure(square + known[2:3])
        powers = [
            square * scale - (total * scale) * (total * scale)
            for total, square in zip(totals, squares)
        ]
        norm = jnp.sqrt(powers[0] + 1e-06) * jnp.sqrt(powers[1] + 1e-06)
        factor = 1.0 / (WIN**3 * WIN**1.5) / norm
        middle_copy(w).wait()

        def second(i, done):
            for j in range(0, 11, 2):
                width = min(2, 11 - j)
                k = i * 11 + j
                values = [
                    spectrum[pl.ds(2 * (k + n), 2)].reshape(2 * WIN, 2 * WIN) for n in range(width)
                ]
                result = mul(t_x[...], stacked(jnp.concatenate(values, axis=1)))
                for n in range(width):
                    part = result[:, 2 * WIN * n : 2 * WIN * (n + 1)]
                    part = jnp.concatenate([part[:WIN], part[WIN:]], axis=1)
                    place = pl.ds(pl.multiple_of((k + n) * WIN, WIN), WIN)
                    high_ref[place, :], low_ref[place, :] = halves(part)
            return done

        lax.fori_loop(0, half // 11, second, 0)

        @pl.when(w + 1 < count)
        def _():
            middle_copy(w + 1).start()

        block = half * WIN // (THIRD * SPLIT)

        def third(i, done):
            for g in range(SPLIT):
                place = pl.ds(pl.multiple_of((i * SPLIT + g) * block, block), block)
                high, low = high_ref[place, :], low_ref[place, :]
                value = mul(jnp.concatenate([high, low, high], axis=1), t_z[...])
                one, two = value[:, : 2 * WIN] * factor, value[:, 2 * WIN :]
                if g == 0:
                    row = lax.broadcasted_iota(jnp.int32, one.shape, 0)
                    column = lax.broadcasted_iota(jnp.int32, one.shape, 1)
                    one = jnp.where((i * block + row == 0) & (column % WIN == 0), 0.0, one)
                cross = jnp.concatenate([one * two, one * pltpu.roll(two, WIN, 1)], axis=1)
                high, low = halves(cross)
                product[place, :] += mul(jnp.concatenate([high, low, high], axis=1), t_iz[w])
            return done

        lax.fori_loop(0, THIRD, third, 0)
        return carry

    lax.fori_loop(0, count, one_window, 0)

    real_lane = lane % (2 * DISP) < DISP

    def fifth(i, done):
        for j in range(11):
            k = i * 11 + j
            value = product[pl.ds(pl.multiple_of(k * WIN, WIN), WIN), :]
            turn = jnp.where(
                real_lane, -pltpu.roll(value, 2 * WIN - DISP, 1), pltpu.roll(value, DISP, 1)
            )
            value = jnp.concatenate([value, turn], axis=0)
            turned[pl.ds(k, DISP, stride=pad), :] = mul(t_ix[...], stacked(value))
        return done

    lax.fori_loop(0, half // 11, fifth, 0)
    for d in range(DISP):
        value = mul(t_iy[...], stacked(turned[d * pad : (d + 1) * pad, :]))
        out[:, d * 2 * WIN : (d + 1) * 2 * WIN] = value[:DISP] - pltpu.roll(
            value[DISP:], 2 * WIN - DISP, 1
        )


def middle_spectra(own, near, far, starts):
    count = starts.shape[0]
    table = window_tables(count)[0]
    vmem = pl.BlockSpec(memory_space=pltpu.VMEM)
    anywhere = pl.BlockSpec(memory_space=pl.ANY)
    return pl.pallas_call(
        functools.partial(middle_body, count),
        out_shape=[
            jax.ShapeDtypeStruct((count, table.shape[0], WIN // 2, 2 * WIN), jnp.float32),
            jax.ShapeDtypeStruct((count, 8, 2 * WIN), jnp.float32),
        ],
        in_specs=[pl.BlockSpec(memory_space=pltpu.SMEM), anywhere, anywhere, anywhere, vmem],
        out_specs=[vmem, vmem],
        scratch_shapes=[
            pltpu.VMEM((3,) + own.shape, jnp.float32),
            pltpu.VMEM((2,) + near.shape, jnp.int16),
            pltpu.SemaphoreType.DMA((3,)),
        ],
        compiler_params=pltpu.CompilerParams(vmem_limit_bytes=LIMIT),
        name="middle",
    )(starts, own, near, far, jnp.asarray(table))


def window_correlations(own, bricks, starts):
    left, right, near, far, *corners = bricks
    middle, stats = middle_spectra(own, near, far, starts)
    bricks = [left, right, *corners]
    count = starts.shape[0]
    tables = window_tables(count)
    half = WIN // 2 + 1
    rows_y = tables[0].shape[0]
    pad = tables[5].shape[1] // 3
    vmem = pl.BlockSpec(memory_space=pltpu.VMEM)
    result = pl.pallas_call(
        functools.partial(window_body, count),
        out_shape=jax.ShapeDtypeStruct((DISP, DISP * 2 * WIN), jnp.float32),
        in_specs=[pl.BlockSpec(memory_space=pltpu.SMEM), vmem]
        + [pl.BlockSpec(memory_space=pl.ANY)] * 7
        + [vmem] * 6,
        out_specs=vmem,
        scratch_shapes=[
            pltpu.VMEM((6,) + own.shape, jnp.float32),
            pltpu.VMEM((6,) + left.shape, jnp.int16),
            pltpu.SemaphoreType.DMA((7,)),
            pltpu.VMEM((rows_y, WIN, 2 * WIN), jnp.float32),
            pltpu.VMEM((half * WIN, 4 * WIN), jnp.bfloat16),
            pltpu.VMEM((half * WIN, 4 * WIN), jnp.bfloat16),
            pltpu.VMEM((half * WIN, 2 * WIN), jnp.float32),
            pltpu.VMEM((DISP * pad, 2 * WIN), jnp.float32),
        ],
        compiler_params=pltpu.CompilerParams(vmem_limit_bytes=WIDE_LIMIT),
        name="windows",
    )(starts, stats, middle, *bricks, *[jnp.asarray(t) for t in tables])
    result = result.reshape(DISP, DISP, 2 * WIN // (2 * DISP), 2 * DISP)[:, :, :count, :DISP]
    return result.transpose(2, 1, 0, 3).reshape(count, DISP**3)


LANES = 128


def chosen_products(value, member, weights_ref):
    count = weights_ref.shape[1]
    half_count = count // 2
    size = weights_ref.shape[2]
    copies = value.shape[0] // member.shape[0]
    total = None
    for start in range(0, half_count, TERMS):
        picked, tables = [], []
        for j in range(start, min(start + TERMS, half_count)):
            hit = (member == j) | (member == j + half_count)
            hit = jnp.concatenate([hit] * copies, axis=0)
            picked.append(jnp.where(hit, value, jnp.zeros_like(value)))
            tables.append(
                jnp.concatenate([weights_ref[0, j], weights_ref[0, j + half_count]], axis=1)
            )
        term = mul(jnp.concatenate(picked, axis=1), jnp.concatenate(tables, axis=0))
        total = term if total is None else total + term
    upper = jnp.concatenate([member.astype(jnp.float32)] * copies, axis=0) >= half_count
    return jnp.where(upper, total[:, size:], total[:, :size])


def placed_tiles(tile, count):
    columns = lax.broadcasted_iota(jnp.int32, tile.shape, 1).astype(jnp.float32)
    columns = columns.astype(tile.dtype)
    one, zero = jnp.ones_like(tile), jnp.zeros_like(tile)
    parts = [
        jnp.where(tile - start == columns, one, zero) for start in range(0, count, LANES)
    ]
    return jnp.concatenate(parts, axis=1)[:, :count]


def sweep_body(back, forward, parity_ref, *refs):
    refs = list(refs)
    volume_ref = refs.pop(0)
    if back:
        own_ratio, other_ratio, back_tile, back_member, back_weights = refs[:5]
        refs = refs[5:]
    if forward:
        next_row, next_member, next_weights = refs[:3]
        refs = refs[3:]
    if back:
        volume_out = refs.pop(0)
    exposures, columns, depth = volume_ref.shape
    block = columns // STEPS
    odd = parity_ref[0] == 1
    if back:
        own, other = own_ratio[...], other_ratio[...]
        ratios = [jnp.where(odd, other, own), jnp.where(odd, own, other)]
        ratios = jnp.concatenate(ratios, axis=1)
    tiles = refs[0].shape[0]

    def one_block(i, total):
        place = pl.ds(pl.multiple_of(i * block, block), block)
        volume = volume_ref[:, place, :].reshape(exposures * block, depth)
        if back:
            placement = placed_tiles(back_tile[0, place, :], own.shape[0])
            spread = mul(placement, ratios).astype(jnp.bfloat16)
            spread = jnp.concatenate(
                [spread[:, e * LANES : (e + 1) * LANES] for e in range(exposures)], axis=0
            )
            member = back_member[0, place, :]
            volume = volume * jnp.exp(chosen_products(spread, member, back_weights))
            volume_out[:, place, :] = volume.reshape(exposures, block, depth)
        if forward:
            member = next_member[0, place, :]
            projected = chosen_products(volume.astype(jnp.bfloat16), member, next_weights)
            parts = list(halves(projected))
            parts = [p[e * block : (e + 1) * block] for p in parts for e in range(exposures)]
            rows = lax.broadcasted_iota(jnp.int32, (tiles, block), 0)
            hit = next_row[0, pl.ds(i, 1), :] == rows
            placement = jnp.where(hit, 1.0, 0.0).astype(jnp.bfloat16)
            value = mul(placement, jnp.concatenate(parts, axis=1))
            size = value.shape[1] // 2
            total = total + (value[:, :size] + value[:, size:])
        return total

    if forward:
        start = jnp.zeros((tiles, exposures * depth), jnp.float32)
        if UNROLL:
            for i in range(STEPS):
                start = one_block(i, start)
            total = start
        else:
            total = lax.fori_loop(0, STEPS, one_block, start)
        kept_ref, sent_ref = refs
        first, second = total[:, :depth], total[:, depth:]
        kept_ref[...] = jnp.where(odd, second, first)
        sent_ref[...] = jnp.where(odd, first, second)
    else:
        lax.fori_loop(0, STEPS, one_block, 0)
        (code_ref,) = refs
        for e in range(exposures):
            logs = jnp.log(jnp.maximum(volume_out[e], 1e-37))
            least = jnp.floor(jnp.min(logs, axis=0, keepdims=True) * GRAIN)
            width = jnp.floor(jnp.max(logs, axis=0, keepdims=True) * GRAIN - least) + 1.0
            rate = (GRAIN * LEVELS) / width
            level = jnp.floor((logs - least / GRAIN) * rate + 0.5) - MIDDLE
            code_ref[e, :columns, :] = level.astype(jnp.int32).astype(jnp.int16)
            row = lax.broadcasted_iota(jnp.int32, (SPARE, depth), 0)
            extra = jnp.where(row == 0, least, jnp.where(row == 1, width, 0.0))
            code_ref[e, columns:, :] = extra.astype(jnp.int32).astype(jnp.int16)


def sweep_step(parity, volume, ratios, columns, weights, weights_turned, tiles, camera, following):
    exposures, count, depth = volume.shape
    pixels = weights.shape[2]
    back, forward = camera is not None, following is not None
    rows, tile_values, members = columns

    def taken(value, index):
        shape = (1,) + value.shape[1:]
        return pl.BlockSpec(shape, lambda i: (index,) + (0,) * (len(shape) - 1))

    def whole(shape):
        return pl.BlockSpec(shape, lambda i: (0,) * len(shape))

    operands = [parity, volume]
    specs = [pl.BlockSpec(memory_space=pltpu.SMEM), whole(volume.shape)]
    shapes = []
    if back:
        operands += [*ratios, tile_values, members, weights]
        specs += [whole((tiles, pixels))] * 2
        specs += [taken(tile_values, camera), taken(members, camera), taken(weights, camera)]
        shapes.append(jax.ShapeDtypeStruct(volume.shape, jnp.float32))
    if forward:
        operands += [rows, members, weights_turned]
        specs += [taken(value, following) for value in operands[-3:]]
        shapes += [jax.ShapeDtypeStruct((tiles, pixels), jnp.float32)] * 2
    else:
        shapes.append(jax.ShapeDtypeStruct((exposures, count + SPARE, depth), jnp.int16))
    result = pl.pallas_call(
        functools.partial(sweep_body, back, forward),
        grid=(1,),
        in_specs=specs,
        out_specs=[whole(value.shape) for value in shapes],
        out_shape=shapes,
        compiler_params=pltpu.CompilerParams(vmem_limit_bytes=LIMIT),
        name="sweep",
    )(*operands)
    return (result[0] if back else volume), (result[-2:] if forward else result[-1])


def column_tables(target, member):
    shape = target.shape + (LANES,)
    tile_values = jnp.broadcast_to(target.astype(jnp.bfloat16)[..., None], shape)
    members = jnp.broadcast_to(member.astype(jnp.bfloat16)[..., None], shape)
    rows = target.reshape(target.shape[0], STEPS, target.shape[1] // STEPS)
    return rows, tile_values, members


def partner_of(count, bit):
    return [(i, i ^ bit) for i in range(count)]


def shared_ratio(kept, sent, picture):
    count = lax.axis_size("wide")
    pair = partner_of(count, 1)
    total = kept + lax.ppermute(sent, "wide", pair)
    bit = 2
    while bit < count:
        total = total + lax.ppermute(total, "wide", partner_of(count, bit))
        bit *= 2
    ratio = (picture - jnp.log(total + 1.0)).astype(jnp.bfloat16)
    return ratio, lax.ppermute(ratio, "wide", pair)


def reconstructed(initial, images, blocks, lib_index, tile_map):
    count = lax.axis_size("wide")
    own_index = lax.axis_index("wide")
    exposures, brick_x, brick_y, depth = initial.shape
    cameras, tile_rows, tile_cols, pixels = images.shape[1:]
    tile_count = tile_rows * tile_cols
    tiles = count * tile_count
    columns = brick_x * brick_y
    strip = own_index - count // 2 + tile_map // tile_count
    target = strip * tile_count + tile_map % tile_count
    missing = -(-tiles // LANES) * LANES
    target = jnp.where((strip >= 0) & (strip < count), target, missing)
    tables = column_tables(
        target.reshape(cameras, columns), lib_index.reshape(cameras, columns)
    )
    parity = (own_index % 2).reshape(1)
    pictures = jnp.log(images.reshape(exposures, cameras, tile_count, pixels) + 1.0)
    by_core = jnp.broadcast_to(pictures[None], (count // 2,) + pictures.shape)
    by_core = by_core.reshape((count, cameras, tile_count, pixels))
    gathered = lax.all_to_all(by_core, "wide", split_axis=0, concat_axis=0, tiled=True)
    gathered = gathered.transpose(1, 0, 2, 3).reshape(cameras, tiles, pixels)
    turned = blocks.transpose(0, 1, 3, 2)
    volume = initial.reshape(exposures, columns, depth)
    order = [camera for _ in range(SWEEPS) for camera in range(cameras)]
    step = functools.partial(
        sweep_step, columns=tables, weights=blocks, weights_turned=turned, tiles=tiles
    )
    volume, partial_value = step(parity, volume, None, camera=None, following=order[0])
    for place, camera in enumerate(order):
        following = order[place + 1] if place + 1 < len(order) else None
        ratios = shared_ratio(*partial_value, gathered[camera])
        volume, partial_value = step(parity, volume, ratios, camera=camera, following=following)
    return volume, partial_value


def neighbours(own):
    def shifted(value, axis, step):
        count = lax.axis_size(axis)
        pairs = [(i, i + step) for i in range(count) if 0 <= i + step < count]
        return lax.ppermute(value, axis, pairs)

    near = shifted(own, "narrow", 1)
    right = shifted(own, "wide", -1)
    far = shifted(own, "narrow", -1)
    left = shifted(own, "wide", 1)
    left_near = shifted(near, "wide", 1)
    right_near = shifted(right, "narrow", 1)
    left_far = shifted(far, "wide", 1)
    right_far = shifted(right, "narrow", -1)
    return [left, right, near, far, left_near, left_far, right_near, right_far]


def body(initial, images, blocks, lib_index, tile_map, win_x, win_y, win_z):
    volume, code = reconstructed(initial, images, blocks, lib_index, tile_map)
    starts = jnp.stack([win_x.reshape(-1), win_y.reshape(-1), win_z.reshape(-1)], axis=1)
    correlation = window_correlations(volume, neighbours(code), starts)
    return (volume.reshape(initial.shape), correlation.reshape(1, 1, starts.shape[0], DISP * DISP * DISP))


def solution(mesh):
    placed = (
        P(None, "wide", "narrow", None),
        P(None, None, "wide", "narrow", None),
        P(),
        P(None, "wide", "narrow"),
        P(None, "wide", "narrow"),
        P("wide", "narrow", None),
        P("wide", "narrow", None),
        P("wide", "narrow", None),
    )
    return jax.shard_map(
        body,
        mesh=mesh,
        in_specs=placed,
        out_specs=(P(None, "wide", "narrow", None), P("wide", "narrow", None, None)),
        check_vma=False,
    )
```

```python
import functools
import numpy as np
import jax
import jax.numpy as jnp
from jax import lax
from jax.experimental import pallas as pl
from jax.experimental.pallas import tpu as pltpu
from jax.sharding import PartitionSpec as P

WIN = 64
DISP = 16
SWEEPS = 2
TERMS = 4
LEVELS = 65535.0
MIDDLE = 32768.0
GRAIN = 16.0
SPARE = 16
LIMIT = 24 * 1024 * 1024
WIDE_LIMIT = 32 * 1024 * 1024
GROUPS = 2
THIRD = 1
SPLIT = 4


def split_table(table):
    high = np.asarray(table, np.float32).astype(jnp.bfloat16)
    low = (np.asarray(table, np.float64) - high.astype(np.float64)).astype(np.float32)
    return high, low.astype(jnp.bfloat16)


def window_tables(count):
    half = WIN // 2 + 1
    unit = 2.0 * np.pi / WIN
    index = np.arange(WIN)
    shifts = np.arange(DISP) - DISP // 2
    turn = unit * np.outer(index, index)
    cos_full, sin_full = np.cos(turn), np.sin(turn)
    rows_y = -(-2 * half // 8) * 8
    first = np.zeros((rows_y, WIN))
    first[0 : 2 * half : 2] = cos_full[:half]
    first[1 : 2 * half : 2] = -sin_full[:half]
    high, low = split_table(first)
    table_y = np.concatenate([high, high, low], axis=1)
    second = np.block([[cos_full, sin_full], [-sin_full, cos_full]])
    high, low = split_table(second)
    table_x = np.concatenate([high, high, low], axis=1)
    third = np.zeros((2, 2, WIN, 2, 2, WIN))
    for e in range(2):
        third[0, e, :, e, 0] = cos_full
        third[1, e, :, e, 0] = sin_full
        third[0, e, :, e, 1] = -sin_full
        third[1, e, :, e, 1] = cos_full
    high, low = split_table(third.reshape(4 * WIN, 4 * WIN))
    table_z = np.concatenate([high, high, low], axis=0)
    part = unit * np.outer(index, shifts)
    cos_part, sin_part = np.cos(part), np.sin(part)
    fourth = np.zeros((4, WIN, 2 * WIN))
    fourth[..., :DISP] = np.stack([cos_part, cos_part, -sin_part, sin_part])
    fourth[..., DISP : 2 * DISP] = np.stack([sin_part, sin_part, cos_part, -cos_part])
    fourth = fourth.reshape(4 * WIN, 2 * WIN)
    shifted = np.stack([np.roll(fourth, w * 2 * DISP, axis=1) for w in range(count)])
    high, low = split_table(shifted)
    table_iz = np.concatenate([high, high, low], axis=1)
    high, low = split_table(np.concatenate([cos_part.T, sin_part.T], axis=1))
    table_ix = np.concatenate([high, high, low], axis=1)
    weight = np.full(half, 2.0)
    weight[0] = weight[-1] = 1.0
    pad = -(-half // 16) * 16
    last = np.zeros((2 * DISP, pad))
    last[:DISP, :half] = cos_part.T[:, :half] * weight
    last[DISP:, :half] = sin_part.T[:, :half] * weight
    high, low = split_table(last)
    table_iy = np.concatenate([high, high, low], axis=1)
    return table_y, table_x, table_z, table_iz, table_ix, table_iy


def halves(value):
    high = value.astype(jnp.bfloat16)
    low = (value - high.astype(jnp.float32)).astype(jnp.bfloat16)
    return high, low


def stacked(value):
    high, low = halves(value)
    return jnp.concatenate([high, low, high], axis=0)


def mul(left, right):
    return jnp.dot(left, right, preferred_element_type=jnp.float32)


def decode(level_ref, target_ref):
    exposures, columns = target_ref.shape[:2]
    for e in range(exposures):
        scale = level_ref[e, columns:, :].astype(jnp.int32).astype(jnp.float32)
        least, width = scale[:1] / GRAIN, scale[1:2]
        step = width / (GRAIN * LEVELS)
        base = least + MIDDLE * step
        present = jnp.where(width > 0.0, 1.0, 0.0)
        for start in range(0, columns, columns // 4):
            place = slice(start, start + columns // 4)
            level = level_ref[e, place, :].astype(jnp.int32).astype(jnp.float32)
            target_ref[e, place, :] = jnp.exp(level * step + base) * present


def first_stage(ext, brick_of, start, mean, table, spectrum_ref):
    half_win = WIN // 2
    _, sy, sz = start
    lane = lax.broadcasted_iota(jnp.int32, (WIN, 2 * WIN), 1)
    row = lax.broadcasted_iota(jnp.int32, (half_win, 2 * WIN), 0)
    left_lane = lane < WIN
    keep = (left_lane & (lane >= sz)) | (~left_lane & (lane < sz + WIN))
    below = row >= sy

    def fold(x):
        brick = brick_of(x)
        inner = pl.ds(pl.multiple_of(x * half_win, half_win), half_win)
        values = []
        for e in range(2):
            low, high = ext[brick, e, inner], ext[brick + 2, e, inner]
            same = ext[brick + 1, e, inner]
            values.append(jnp.concatenate([jnp.where(below, low, high), same], axis=0))
        stay = jnp.where(left_lane, values[0], values[1])
        move = jnp.where(left_lane, values[1], values[0])
        return jnp.where(keep, stay, pltpu.roll(move, WIN, 1)) - mean

    def one_group(i, sums):
        total, square = sums
        for g in range(GROUPS):
            begin = (i * GROUPS + g) * 8
            results = []
            for j in range(0, 8, 2):
                values = [fold(begin + j + k) for k in range(2)]
                for value in values:
                    total = total + value
                    square = square + value * value
                result = mul(table, stacked(jnp.concatenate(values, axis=1)))
                results += [result[:, : 2 * WIN], result[:, 2 * WIN :]]
            spectrum_ref[:, pl.ds(pl.multiple_of(begin, 8), 8), :] = jnp.swapaxes(
                jnp.stack(results), 0, 1
            )
        return total, square

    zero = jnp.zeros((WIN, 2 * WIN), jnp.float32)
    total, square = lax.fori_loop(0, half_win // (8 * GROUPS), one_group, (zero, zero))
    return [jnp.sum(value, axis=0, keepdims=True) for value in (total, square)]


def by_exposure(value):
    left = lax.broadcasted_iota(jnp.int32, value.shape, 1) < WIN
    return (
        jnp.sum(jnp.where(left, value, 0.0), axis=1, keepdims=True),
        jnp.sum(jnp.where(left, 0.0, value), axis=1, keepdims=True),
    )


def middle_body(count, starts, own, near, far, t_y, spectrum_out, stats_out, ext, levels, sems):
    copies = [
        pltpu.make_async_copy(source, target, sems.at[i])
        for i, (source, target) in enumerate(
            [(own, ext.at[1]), (near, levels.at[0]), (far, levels.at[1])]
        )
    ]
    for copy in copies:
        copy.start()
    for copy in copies:
        copy.wait()
    decode(levels.at[0], ext.at[0])
    decode(levels.at[1], ext.at[2])
    exposures, columns, depth = ext.shape[1:]
    sums = [jnp.sum(ext[1, e], axis=0, keepdims=True) for e in range(exposures)]
    lane = lax.broadcasted_iota(jnp.int32, (1, depth), 1)

    def one_window(w, done):
        start = [starts[w, n] for n in range(3)]
        inside = (lane >= start[2]) & (lane < start[2] + WIN)
        means = [
            jnp.sum(jnp.where(inside, value, 0.0), axis=1, keepdims=True) / (columns * WIN)
            for value in sums
        ]
        mean = jnp.where(lane < WIN, means[0], means[1])
        total, square = first_stage(
            ext, lambda x: 0, start, mean, t_y[...], spectrum_out.at[w]
        )
        spare = jnp.zeros((5, depth), jnp.float32)
        stats_out[w] = jnp.concatenate([mean, total, square, spare], axis=0)
        return done

    lax.fori_loop(0, count, one_window, 0)


def window_body(count, starts, stats, *refs):
    middle, left, right, left_near, left_far, right_near, right_far = refs[:7]
    t_y, t_x, t_z, t_iz, t_ix, t_iy, out = refs[7:14]
    ext, levels, sems, spectrum, high_ref, low_ref, product, turned = refs[14:]
    half = WIN // 2 + 1
    pad = t_iy.shape[1] // 3
    sources = [left_near, left, left_far, right_near, right, right_far]
    copies = [
        pltpu.make_async_copy(source, levels.at[i], sems.at[i])
        for i, source in enumerate(sources)
    ]

    def middle_copy(w):
        target = spectrum.at[:, pl.ds(WIN // 2, WIN // 2), :]
        return pltpu.make_async_copy(middle.at[w], target, sems.at[len(sources)])

    middle_copy(0).start()
    for copy in copies:
        copy.start()
    product[...] = jnp.zeros_like(product)
    turned[...] = jnp.zeros_like(turned)
    for copy in copies:
        copy.wait()

    def decode_one(i, done):
        decode(levels.at[i], ext.at[i])
        return done

    lax.fori_loop(0, len(sources), decode_one, 0)
    lane = lax.broadcasted_iota(jnp.int32, (WIN, 2 * WIN), 1)

    def one_window(w, carry):
        start = [starts[w, n] for n in range(3)]
        known = stats[w]
        total, square = first_stage(
            ext,
            lambda x: jnp.where(x >= start[0], 0, 3),
            start,
            known[:1],
            t_y[...],
            spectrum,
        )
        scale = 1.0 / WIN**3
        totals, squares = by_exposure(total + known[1:2]), by_exposure(square + known[2:3])
        powers = [
            square * scale - (total * scale) * (total * scale)
            for total, square in zip(totals, squares)
        ]
        norm = jnp.sqrt(powers[0] + 1e-06) * jnp.sqrt(powers[1] + 1e-06)
        factor = 1.0 / (WIN**3 * WIN**1.5) / norm
        middle_copy(w).wait()

        def second(i, done):
            for j in range(0, 11, 2):
                width = min(2, 11 - j)
                k = i * 11 + j
                values = [
                    spectrum[pl.ds(2 * (k + n), 2)].reshape(2 * WIN, 2 * WIN) for n in range(width)
                ]
                result = mul(t_x[...], stacked(jnp.concatenate(values, axis=1)))
                for n in range(width):
                    part = result[:, 2 * WIN * n : 2 * WIN * (n + 1)]
                    part = jnp.concatenate([part[:WIN], part[WIN:]], axis=1)
                    place = pl.ds(pl.multiple_of((k + n) * WIN, WIN), WIN)
                    high_ref[place, :], low_ref[place, :] = halves(part)
            return done

        lax.fori_loop(0, half // 11, second, 0)

        @pl.when(w + 1 < count)
        def _():
            middle_copy(w + 1).start()

        block = half * WIN // (THIRD * SPLIT)

        def third(i, done):
            for g in range(SPLIT):
                place = pl.ds(pl.multiple_of((i * SPLIT + g) * block, block), block)
                high, low = high_ref[place, :], low_ref[place, :]
                value = mul(jnp.concatenate([high, low, high], axis=1), t_z[...])
                one, two = value[:, : 2 * WIN] * factor, value[:, 2 * WIN :]
                if g == 0:
                    row = lax.broadcasted_iota(jnp.int32, one.shape, 0)
                    column = lax.broadcasted_iota(jnp.int32, one.shape, 1)
                    one = jnp.where((i * block + row == 0) & (column % WIN == 0), 0.0, one)
                cross = jnp.concatenate([one * two, one * pltpu.roll(two, WIN, 1)], axis=1)
                high, low = halves(cross)
                product[place, :] += mul(jnp.concatenate([high, low, high], axis=1), t_iz[w])
            return done

        lax.fori_loop(0, THIRD, third, 0)
        return carry

    lax.fori_loop(0, count, one_window, 0)

    real_lane = lane % (2 * DISP) < DISP

    def fifth(i, done):
        for j in range(11):
            k = i * 11 + j
            value = product[pl.ds(pl.multiple_of(k * WIN, WIN), WIN), :]
            turn = jnp.where(
                real_lane, -pltpu.roll(value, 2 * WIN - DISP, 1), pltpu.roll(value, DISP, 1)
            )
            value = jnp.concatenate([value, turn], axis=0)
            turned[pl.ds(k, DISP, stride=pad), :] = mul(t_ix[...], stacked(value))
        return done

    lax.fori_loop(0, half // 11, fifth, 0)
    for d in range(DISP):
        value = mul(t_iy[...], stacked(turned[d * pad : (d + 1) * pad, :]))
        out[:, d * 2 * WIN : (d + 1) * 2 * WIN] = value[:DISP] - pltpu.roll(
            value[DISP:], 2 * WIN - DISP, 1
        )


def middle_spectra(own, near, far, starts):
    count = starts.shape[0]
    table = window_tables(count)[0]
    vmem = pl.BlockSpec(memory_space=pltpu.VMEM)
    anywhere = pl.BlockSpec(memory_space=pl.ANY)
    return pl.pallas_call(
        functools.partial(middle_body, count),
        out_shape=[
            jax.ShapeDtypeStruct((count, table.shape[0], WIN // 2, 2 * WIN), jnp.float32),
            jax.ShapeDtypeStruct((count, 8, 2 * WIN), jnp.float32),
        ],
        in_specs=[pl.BlockSpec(memory_space=pltpu.SMEM), anywhere, anywhere, anywhere, vmem],
        out_specs=[vmem, vmem],
        scratch_shapes=[
            pltpu.VMEM((3,) + own.shape, jnp.float32),
            pltpu.VMEM((2,) + near.shape, jnp.int16),
            pltpu.SemaphoreType.DMA((3,)),
        ],
        compiler_params=pltpu.CompilerParams(vmem_limit_bytes=LIMIT),
        name="middle",
    )(starts, own, near, far, jnp.asarray(table))


def window_correlations(own, bricks, starts):
    left, right, near, far, *corners = bricks
    middle, stats = middle_spectra(own, near, far, starts)
    bricks = [left, right, *corners]
    count = starts.shape[0]
    tables = window_tables(count)
    half = WIN // 2 + 1
    rows_y = tables[0].shape[0]
    pad = tables[5].shape[1] // 3
    vmem = pl.BlockSpec(memory_space=pltpu.VMEM)
    result = pl.pallas_call(
        functools.partial(window_body, count),
        out_shape=jax.ShapeDtypeStruct((DISP, DISP * 2 * WIN), jnp.float32),
        in_specs=[pl.BlockSpec(memory_space=pltpu.SMEM), vmem]
        + [pl.BlockSpec(memory_space=pl.ANY)] * 7
        + [vmem] * 6,
        out_specs=vmem,
        scratch_shapes=[
            pltpu.VMEM((6,) + own.shape, jnp.float32),
            pltpu.VMEM((6,) + left.shape, jnp.int16),
            pltpu.SemaphoreType.DMA((7,)),
            pltpu.VMEM((rows_y, WIN, 2 * WIN), jnp.float32),
            pltpu.VMEM((half * WIN, 4 * WIN), jnp.bfloat16),
            pltpu.VMEM((half * WIN, 4 * WIN), jnp.bfloat16),
            pltpu.VMEM((half * WIN, 2 * WIN), jnp.float32),
            pltpu.VMEM((DISP * pad, 2 * WIN), jnp.float32),
        ],
        compiler_params=pltpu.CompilerParams(vmem_limit_bytes=WIDE_LIMIT),
        name="windows",
    )(starts, stats, middle, *bricks, *[jnp.asarray(t) for t in tables])
    result = result.reshape(DISP, DISP, 2 * WIN // (2 * DISP), 2 * DISP)[:, :, :count, :DISP]
    return result.transpose(2, 1, 0, 3).reshape(count, DISP**3)


LANES = 128


def chosen_products(value, member, weights_ref):
    count = weights_ref.shape[1]
    half_count = count // 2
    size = weights_ref.shape[2]
    copies = value.shape[0] // member.shape[0]
    total = None
    for start in range(0, half_count, TERMS):
        picked, tables = [], []
        for j in range(start, min(start + TERMS, half_count)):
            hit = (member == j) | (member == j + half_count)
            hit = jnp.concatenate([hit] * copies, axis=0)
            picked.append(jnp.where(hit, value, jnp.zeros_like(value)))
            tables.append(
                jnp.concatenate([weights_ref[0, j], weights_ref[0, j + half_count]], axis=1)
            )
        term = mul(jnp.concatenate(picked, axis=1), jnp.concatenate(tables, axis=0))
        total = term if total is None else total + term
    upper = jnp.concatenate([member.astype(jnp.float32)] * copies, axis=0) >= half_count
    return jnp.where(upper, total[:, size:], total[:, :size])


def placed_tiles(tile, count):
    columns = lax.broadcasted_iota(jnp.int32, tile.shape, 1).astype(jnp.float32)
    columns = columns.astype(tile.dtype)
    one, zero = jnp.ones_like(tile), jnp.zeros_like(tile)
    parts = [
        jnp.where(tile - start == columns, one, zero) for start in range(0, count, LANES)
    ]
    return jnp.concatenate(parts, axis=1)[:, :count]


def updated(volume, ratio, tile, member, weights_ref):
    placement = placed_tiles(tile, ratio.shape[0])
    spread = mul(placement, ratio).astype(jnp.bfloat16)
    return volume * jnp.exp(chosen_products(spread, member, weights_ref))


def sweep_body(back, forward, volume_ref, *refs):
    refs = list(refs)
    if back:
        ratio_ref, back_tile, back_member, back_weights = refs[:4]
        refs = refs[4:]
    if forward:
        next_row, next_member, next_weights = refs[:3]
        refs = refs[3:]
    volume = volume_ref[...]
    if back:
        volume = updated(volume, ratio_ref[...], back_tile[0], back_member[0], back_weights)
        refs.pop(0)[...] = volume
    if forward:
        (partial_ref,) = refs
        tiles = partial_ref.shape[0]
        projected = chosen_products(volume.astype(jnp.bfloat16), next_member[0], next_weights)
        rows = lax.broadcasted_iota(jnp.int32, (tiles, volume.shape[0]), 0)
        placement = jnp.where(next_row[0] == rows, 1.0, 0.0).astype(jnp.bfloat16)
        value = mul(placement, jnp.concatenate(halves(projected), axis=1))
        size = value.shape[1] // 2
        partial_ref[...] = value[:, :size] + value[:, size:]


def last_body(parity_ref, *refs):
    kept, other, own_ratio, other_ratio, tile, member, weights, volume_out, code_out = refs
    columns, depth = kept.shape
    parity = parity_ref[0]
    pairs = ((parity, kept, own_ratio), (1 - parity, other, other_ratio))
    for e, volume_ref, ratio_ref in pairs:
        volume = updated(volume_ref[...], ratio_ref[...], tile[0], member[0], weights)
        volume_out[e] = volume
        logs = jnp.log(jnp.maximum(volume, 1e-37))
        least = jnp.floor(jnp.min(logs, axis=0, keepdims=True) * GRAIN)
        width = jnp.floor(jnp.max(logs, axis=0, keepdims=True) * GRAIN - least) + 1.0
        rate = (GRAIN * LEVELS) / width
        level = jnp.floor((logs - least / GRAIN) * rate + 0.5) - MIDDLE
        code_out[e, :columns, :] = level.astype(jnp.int32).astype(jnp.int16)
        row = lax.broadcasted_iota(jnp.int32, (SPARE, depth), 0)
        extra = jnp.where(row == 0, least, jnp.where(row == 1, width, 0.0))
        code_out[e, columns:, :] = extra.astype(jnp.int32).astype(jnp.int16)


def taken(value, index):
    shape = (1,) + value.shape[1:]
    return pl.BlockSpec(shape, lambda i: (index,) + (0,) * (len(shape) - 1))


def whole(value):
    return pl.BlockSpec(value.shape, lambda i: (0,) * len(value.shape))


def sweep_step(volume, ratio, columns, weights, weights_turned, tiles, camera, following):
    back, forward = camera is not None, following is not None
    rows, tile_values, members = columns
    operands, specs, shapes = [volume], [whole(volume)], []
    if back:
        operands += [ratio, tile_values, members, weights]
        specs += [whole(ratio)] + [taken(value, camera) for value in operands[-3:]]
        shapes.append(jax.ShapeDtypeStruct(volume.shape, jnp.float32))
    if forward:
        operands += [rows, members, weights_turned]
        specs += [taken(value, following) for value in operands[-3:]]
        shapes.append(jax.ShapeDtypeStruct((tiles, weights.shape[2]), jnp.float32))
    return pl.pallas_call(
        functools.partial(sweep_body, back, forward),
        grid=(1,),
        in_specs=specs,
        out_specs=[whole(value) for value in shapes],
        out_shape=shapes,
        compiler_params=pltpu.CompilerParams(vmem_limit_bytes=LIMIT),
        name="sweep",
    )(*operands)


def last_step(parity, volumes, ratios, columns, weights, camera):
    count, depth = volumes[0].shape
    exposures = len(volumes)
    tables = [columns[1], columns[2], weights]
    shapes = [
        jax.ShapeDtypeStruct((exposures, count, depth), jnp.float32),
        jax.ShapeDtypeStruct((exposures, count + SPARE, depth), jnp.int16),
    ]
    return pl.pallas_call(
        last_body,
        grid=(1,),
        in_specs=[pl.BlockSpec(memory_space=pltpu.SMEM)]
        + [whole(value) for value in (*volumes, *ratios)]
        + [taken(value, camera) for value in tables],
        out_specs=[whole(value) for value in shapes],
        out_shape=shapes,
        compiler_params=pltpu.CompilerParams(vmem_limit_bytes=LIMIT),
        name="last",
    )(parity, *volumes, *ratios, *tables)


def column_tables(target, member):
    shape = target.shape + (LANES,)
    tile_values = jnp.broadcast_to(target.astype(jnp.bfloat16)[..., None], shape)
    members = jnp.broadcast_to(member.astype(jnp.bfloat16)[..., None], shape)
    return target[:, None, :], tile_values, members


def partner_of(count, bit):
    return [(i, i ^ bit) for i in range(count)]


def shared_ratio(total, picture):
    count = lax.axis_size("wide")
    bit = 2
    while bit < count:
        total = total + lax.ppermute(total, "wide", partner_of(count, bit))
        bit *= 2
    return (picture - jnp.log(total + 1.0)).astype(jnp.bfloat16)


def reconstructed(initial, images, blocks, lib_index, tile_map):
    count = lax.axis_size("wide")
    own_index = lax.axis_index("wide")
    exposures, brick_x, brick_y, depth = initial.shape
    cameras, tile_rows, tile_cols, pixels = images.shape[1:]
    tile_count = tile_rows * tile_cols
    tiles = count * tile_count
    columns = brick_x * brick_y
    strip = own_index - count // 2 + tile_map // tile_count
    target = strip * tile_count + tile_map % tile_count
    missing = -(-tiles // LANES) * LANES
    target = jnp.where((strip >= 0) & (strip < count), target, missing)
    tables = column_tables(
        target.reshape(cameras, columns), lib_index.reshape(cameras, columns)
    )
    parity = own_index % 2
    pictures = jnp.log(images.reshape(exposures, cameras, tile_count, pixels) + 1.0)
    by_core = jnp.broadcast_to(pictures[None], (count // 2,) + pictures.shape)
    by_core = by_core.reshape((count, cameras, tile_count, pixels))
    gathered = lax.all_to_all(by_core, "wide", split_axis=0, concat_axis=0, tiled=True)
    gathered = gathered.transpose(1, 0, 2, 3).reshape(cameras, tiles, pixels)
    turned = blocks.transpose(0, 1, 3, 2)
    volume = initial.reshape(exposures, columns, depth)
    kept = lax.dynamic_index_in_dim(volume, parity, 0, keepdims=False)
    other = lax.dynamic_index_in_dim(volume, 1 - parity, 0, keepdims=False)
    order = [camera for _ in range(SWEEPS) for camera in range(cameras)]
    step = functools.partial(
        sweep_step, columns=tables, weights=blocks, weights_turned=turned, tiles=tiles
    )

    def swapped(value):
        return lax.ppermute(value, "wide", partner_of(count, 1))

    (sent,) = step(other, None, camera=None, following=order[0])
    (own,) = step(kept, None, camera=None, following=order[0])
    for camera, following in zip(order, order[1:]):
        ratio = shared_ratio(own + swapped(sent), gathered[camera])
        other_ratio = swapped(ratio)
        (kept,) = step(kept, ratio, camera=camera, following=None)
        other, sent = step(other, other_ratio, camera=camera, following=following)
        (own,) = step(kept, None, camera=None, following=following)
    ratio = shared_ratio(own + swapped(sent), gathered[order[-1]])
    return last_step(
        parity.reshape(1), (kept, other), (ratio, swapped(ratio)), tables, blocks, order[-1]
    )


def neighbours(own):
    def shifted(value, axis, step):
        count = lax.axis_size(axis)
        pairs = [(i, i + step) for i in range(count) if 0 <= i + step < count]
        return lax.ppermute(value, axis, pairs)

    near = shifted(own, "narrow", 1)
    right = shifted(own, "wide", -1)
    far = shifted(own, "narrow", -1)
    left = shifted(own, "wide", 1)
    left_near = shifted(near, "wide", 1)
    right_near = shifted(right, "narrow", 1)
    left_far = shifted(far, "wide", 1)
    right_far = shifted(right, "narrow", -1)
    return [left, right, near, far, left_near, left_far, right_near, right_far]


def body(initial, images, blocks, lib_index, tile_map, win_x, win_y, win_z):
    volume, code = reconstructed(initial, images, blocks, lib_index, tile_map)
    starts = jnp.stack([win_x.reshape(-1), win_y.reshape(-1), win_z.reshape(-1)], axis=1)
    correlation = window_correlations(volume, neighbours(code), starts)
    return (volume.reshape(initial.shape), correlation.reshape(1, 1, starts.shape[0], DISP * DISP * DISP))


def solution(mesh):
    placed = (
        P(None, "wide", "narrow", None),
        P(None, None, "wide", "narrow", None),
        P(),
        P(None, "wide", "narrow"),
        P(None, "wide", "narrow"),
        P("wide", "narrow", None),
        P("wide", "narrow", None),
        P("wide", "narrow", None),
    )
    return jax.shard_map(
        body,
        mesh=mesh,
        in_specs=placed,
        out_specs=(P(None, "wide", "narrow", None), P("wide", "narrow", None, None)),
        check_vma=False,
    )
```

```python
import functools
import numpy as np
import jax
import jax.numpy as jnp
from jax import lax
from jax.experimental import pallas as pl
from jax.experimental.pallas import tpu as pltpu
from jax.sharding import PartitionSpec as P

WIN = 64
DISP = 16
SWEEPS = 2
TERMS = 4
LEVELS = 65535.0
MIDDLE = 32768.0
GRAIN = 16.0
SPARE = 16
LIMIT = 24 * 1024 * 1024
WIDE_LIMIT = 32 * 1024 * 1024
GROUPS = 2
THIRD = 1
SPLIT = 4


def split_table(table):
    high = np.asarray(table, np.float32).astype(jnp.bfloat16)
    low = (np.asarray(table, np.float64) - high.astype(np.float64)).astype(np.float32)
    return high, low.astype(jnp.bfloat16)


def window_tables(count):
    half = WIN // 2 + 1
    unit = 2.0 * np.pi / WIN
    index = np.arange(WIN)
    shifts = np.arange(DISP) - DISP // 2
    turn = unit * np.outer(index, index)
    cos_full, sin_full = np.cos(turn), np.sin(turn)
    rows_y = -(-2 * half // 8) * 8
    first = np.zeros((rows_y, WIN))
    first[0 : 2 * half : 2] = cos_full[:half]
    first[1 : 2 * half : 2] = -sin_full[:half]
    high, low = split_table(first)
    table_y = np.concatenate([high, high, low], axis=1)
    second = np.block([[cos_full, sin_full], [-sin_full, cos_full]])
    high, low = split_table(second)
    table_x = np.concatenate([high, high, low], axis=1)
    third = np.zeros((2, 2, WIN, 2, 2, WIN))
    for e in range(2):
        third[0, e, :, e, 0] = cos_full
        third[1, e, :, e, 0] = sin_full
        third[0, e, :, e, 1] = -sin_full
        third[1, e, :, e, 1] = cos_full
    high, low = split_table(third.reshape(4 * WIN, 4 * WIN))
    table_z = np.concatenate([high, high, low], axis=0)
    part = unit * np.outer(index, shifts)
    cos_part, sin_part = np.cos(part), np.sin(part)
    fourth = np.zeros((4, WIN, 2 * WIN))
    fourth[..., :DISP] = np.stack([cos_part, cos_part, -sin_part, sin_part])
    fourth[..., DISP : 2 * DISP] = np.stack([sin_part, sin_part, cos_part, -cos_part])
    fourth = fourth.reshape(4 * WIN, 2 * WIN)
    shifted = np.stack([np.roll(fourth, w * 2 * DISP, axis=1) for w in range(count)])
    high, low = split_table(shifted)
    table_iz = np.concatenate([high, high, low], axis=1)
    high, low = split_table(np.concatenate([cos_part.T, sin_part.T], axis=1))
    table_ix = np.concatenate([high, high, low], axis=1)
    weight = np.full(half, 2.0)
    weight[0] = weight[-1] = 1.0
    pad = -(-half // 16) * 16
    last = np.zeros((2 * DISP, pad))
    last[:DISP, :half] = cos_part.T[:, :half] * weight
    last[DISP:, :half] = sin_part.T[:, :half] * weight
    high, low = split_table(last)
    table_iy = np.concatenate([high, high, low], axis=1)
    return table_y, table_x, table_z, table_iz, table_ix, table_iy


def halves(value):
    high = value.astype(jnp.bfloat16)
    low = (value - high.astype(jnp.float32)).astype(jnp.bfloat16)
    return high, low


def stacked(value):
    high, low = halves(value)
    return jnp.concatenate([high, low, high], axis=0)


def mul(left, right):
    return jnp.dot(left, right, preferred_element_type=jnp.float32)


def decode(level_ref, target_ref):
    exposures, columns = target_ref.shape[:2]
    for e in range(exposures):
        scale = level_ref[e, columns:, :].astype(jnp.int32).astype(jnp.float32)
        least, width = scale[:1] / GRAIN, scale[1:2]
        step = width / (GRAIN * LEVELS)
        base = least + MIDDLE * step
        present = jnp.where(width > 0.0, 1.0, 0.0)
        for start in range(0, columns, columns // 4):
            place = slice(start, start + columns // 4)
            level = level_ref[e, place, :].astype(jnp.int32).astype(jnp.float32)
            target_ref[e, place, :] = jnp.exp(level * step + base) * present


def first_stage(ext, brick_of, start, mean, table, spectrum_ref):
    half_win = WIN // 2
    _, sy, sz = start
    lane = lax.broadcasted_iota(jnp.int32, (WIN, 2 * WIN), 1)
    row = lax.broadcasted_iota(jnp.int32, (half_win, 2 * WIN), 0)
    left_lane = lane < WIN
    keep = (left_lane & (lane >= sz)) | (~left_lane & (lane < sz + WIN))
    below = row >= sy

    def fold(x):
        brick = brick_of(x)
        inner = pl.ds(pl.multiple_of(x * half_win, half_win), half_win)
        values = []
        for e in range(2):
            low, high = ext[brick, e, inner], ext[brick + 2, e, inner]
            same = ext[brick + 1, e, inner]
            values.append(jnp.concatenate([jnp.where(below, low, high), same], axis=0))
        stay = jnp.where(left_lane, values[0], values[1])
        move = jnp.where(left_lane, values[1], values[0])
        return jnp.where(keep, stay, pltpu.roll(move, WIN, 1)) - mean

    def one_group(i, sums):
        total, square = sums
        for g in range(GROUPS):
            begin = (i * GROUPS + g) * 8
            results = []
            for j in range(0, 8, 2):
                values = [fold(begin + j + k) for k in range(2)]
                for value in values:
                    total = total + value
                    square = square + value * value
                result = mul(table, stacked(jnp.concatenate(values, axis=1)))
                results += [result[:, : 2 * WIN], result[:, 2 * WIN :]]
            spectrum_ref[:, pl.ds(pl.multiple_of(begin, 8), 8), :] = jnp.swapaxes(
                jnp.stack(results), 0, 1
            )
        return total, square

    zero = jnp.zeros((WIN, 2 * WIN), jnp.float32)
    total, square = lax.fori_loop(0, half_win // (8 * GROUPS), one_group, (zero, zero))
    return [jnp.sum(value, axis=0, keepdims=True) for value in (total, square)]


def by_exposure(value):
    left = lax.broadcasted_iota(jnp.int32, value.shape, 1) < WIN
    return (
        jnp.sum(jnp.where(left, value, 0.0), axis=1, keepdims=True),
        jnp.sum(jnp.where(left, 0.0, value), axis=1, keepdims=True),
    )


def middle_body(count, starts, own, near, far, t_y, spectrum_out, stats_out, ext, levels, sems):
    copies = [
        pltpu.make_async_copy(source, target, sems.at[i])
        for i, (source, target) in enumerate(
            [(own, ext.at[1]), (near, levels.at[0]), (far, levels.at[1])]
        )
    ]
    for copy in copies:
        copy.start()
    for copy in copies:
        copy.wait()
    decode(levels.at[0], ext.at[0])
    decode(levels.at[1], ext.at[2])
    exposures, columns, depth = ext.shape[1:]
    sums = [jnp.sum(ext[1, e], axis=0, keepdims=True) for e in range(exposures)]
    lane = lax.broadcasted_iota(jnp.int32, (1, depth), 1)

    def one_window(w, done):
        start = [starts[w, n] for n in range(3)]
        inside = (lane >= start[2]) & (lane < start[2] + WIN)
        means = [
            jnp.sum(jnp.where(inside, value, 0.0), axis=1, keepdims=True) / (columns * WIN)
            for value in sums
        ]
        mean = jnp.where(lane < WIN, means[0], means[1])
        total, square = first_stage(
            ext, lambda x: 0, start, mean, t_y[...], spectrum_out.at[w]
        )
        spare = jnp.zeros((5, depth), jnp.float32)
        stats_out[w] = jnp.concatenate([mean, total, square, spare], axis=0)
        return done

    lax.fori_loop(0, count, one_window, 0)


def window_body(count, starts, stats, *refs):
    middle, left, right, left_near, left_far, right_near, right_far = refs[:7]
    t_y, t_x, t_z, t_iz, t_ix, t_iy, out = refs[7:14]
    ext, levels, sems, spectrum, high_ref, low_ref, product, turned = refs[14:]
    half = WIN // 2 + 1
    pad = t_iy.shape[1] // 3
    sources = [left_near, left, left_far, right_near, right, right_far]
    copies = [
        pltpu.make_async_copy(source, levels.at[i], sems.at[i])
        for i, source in enumerate(sources)
    ]

    def middle_copy(w):
        target = spectrum.at[:, pl.ds(WIN // 2, WIN // 2), :]
        return pltpu.make_async_copy(middle.at[w], target, sems.at[len(sources)])

    middle_copy(0).start()
    for copy in copies:
        copy.start()
    product[...] = jnp.zeros_like(product)
    turned[...] = jnp.zeros_like(turned)
    for copy in copies:
        copy.wait()

    def decode_one(i, done):
        decode(levels.at[i], ext.at[i])
        return done

    lax.fori_loop(0, len(sources), decode_one, 0)
    lane = lax.broadcasted_iota(jnp.int32, (WIN, 2 * WIN), 1)

    def one_window(w, carry):
        start = [starts[w, n] for n in range(3)]
        known = stats[w]
        total, square = first_stage(
            ext,
            lambda x: jnp.where(x >= start[0], 0, 3),
            start,
            known[:1],
            t_y[...],
            spectrum,
        )
        scale = 1.0 / WIN**3
        totals, squares = by_exposure(total + known[1:2]), by_exposure(square + known[2:3])
        powers = [
            square * scale - (total * scale) * (total * scale)
            for total, square in zip(totals, squares)
        ]
        norm = jnp.sqrt(powers[0] + 1e-06) * jnp.sqrt(powers[1] + 1e-06)
        factor = 1.0 / (WIN**3 * WIN**1.5) / norm
        middle_copy(w).wait()

        def second(i, done):
            for j in range(0, 11, 2):
                width = min(2, 11 - j)
                k = i * 11 + j
                values = [
                    spectrum[pl.ds(2 * (k + n), 2)].reshape(2 * WIN, 2 * WIN) for n in range(width)
                ]
                result = mul(t_x[...], stacked(jnp.concatenate(values, axis=1)))
                for n in range(width):
                    part = result[:, 2 * WIN * n : 2 * WIN * (n + 1)]
                    part = jnp.concatenate([part[:WIN], part[WIN:]], axis=1)
                    place = pl.ds(pl.multiple_of((k + n) * WIN, WIN), WIN)
                    high_ref[place, :], low_ref[place, :] = halves(part)
            return done

        lax.fori_loop(0, half // 11, second, 0)

        @pl.when(w + 1 < count)
        def _():
            middle_copy(w + 1).start()

        block = half * WIN // (THIRD * SPLIT)

        def third(i, done):
            for g in range(SPLIT):
                place = pl.ds(pl.multiple_of((i * SPLIT + g) * block, block), block)
                high, low = high_ref[place, :], low_ref[place, :]
                value = mul(jnp.concatenate([high, low, high], axis=1), t_z[...])
                one, two = value[:, : 2 * WIN] * factor, value[:, 2 * WIN :]
                if g == 0:
                    row = lax.broadcasted_iota(jnp.int32, one.shape, 0)
                    column = lax.broadcasted_iota(jnp.int32, one.shape, 1)
                    one = jnp.where((i * block + row == 0) & (column % WIN == 0), 0.0, one)
                cross = jnp.concatenate([one * two, one * pltpu.roll(two, WIN, 1)], axis=1)
                high, low = halves(cross)
                product[place, :] += mul(jnp.concatenate([high, low, high], axis=1), t_iz[w])
            return done

        lax.fori_loop(0, THIRD, third, 0)
        return carry

    lax.fori_loop(0, count, one_window, 0)

    real_lane = lane % (2 * DISP) < DISP

    def fifth(i, done):
        for j in range(11):
            k = i * 11 + j
            value = product[pl.ds(pl.multiple_of(k * WIN, WIN), WIN), :]
            turn = jnp.where(
                real_lane, -pltpu.roll(value, 2 * WIN - DISP, 1), pltpu.roll(value, DISP, 1)
            )
            value = jnp.concatenate([value, turn], axis=0)
            turned[pl.ds(k, DISP, stride=pad), :] = mul(t_ix[...], stacked(value))
        return done

    lax.fori_loop(0, half // 11, fifth, 0)
    for d in range(DISP):
        value = mul(t_iy[...], stacked(turned[d * pad : (d + 1) * pad, :]))
        out[:, d * 2 * WIN : (d + 1) * 2 * WIN] = value[:DISP] - pltpu.roll(
            value[DISP:], 2 * WIN - DISP, 1
        )


def middle_spectra(own, near, far, starts):
    count = starts.shape[0]
    table = window_tables(count)[0]
    vmem = pl.BlockSpec(memory_space=pltpu.VMEM)
    anywhere = pl.BlockSpec(memory_space=pl.ANY)
    return pl.pallas_call(
        functools.partial(middle_body, count),
        out_shape=[
            jax.ShapeDtypeStruct((count, table.shape[0], WIN // 2, 2 * WIN), jnp.float32),
            jax.ShapeDtypeStruct((count, 8, 2 * WIN), jnp.float32),
        ],
        in_specs=[pl.BlockSpec(memory_space=pltpu.SMEM), anywhere, anywhere, anywhere, vmem],
        out_specs=[vmem, vmem],
        scratch_shapes=[
            pltpu.VMEM((3,) + own.shape, jnp.float32),
            pltpu.VMEM((2,) + near.shape, jnp.int16),
            pltpu.SemaphoreType.DMA((3,)),
        ],
        compiler_params=pltpu.CompilerParams(vmem_limit_bytes=LIMIT),
        name="middle",
    )(starts, own, near, far, jnp.asarray(table))


def window_correlations(own, bricks, starts):
    left, right, near, far, *corners = bricks
    middle, stats = middle_spectra(own, near, far, starts)
    bricks = [left, right, *corners]
    count = starts.shape[0]
    tables = window_tables(count)
    half = WIN // 2 + 1
    rows_y = tables[0].shape[0]
    pad = tables[5].shape[1] // 3
    vmem = pl.BlockSpec(memory_space=pltpu.VMEM)
    result = pl.pallas_call(
        functools.partial(window_body, count),
        out_shape=jax.ShapeDtypeStruct((DISP, DISP * 2 * WIN), jnp.float32),
        in_specs=[pl.BlockSpec(memory_space=pltpu.SMEM), vmem]
        + [pl.BlockSpec(memory_space=pl.ANY)] * 7
        + [vmem] * 6,
        out_specs=vmem,
        scratch_shapes=[
            pltpu.VMEM((6,) + own.shape, jnp.float32),
            pltpu.VMEM((6,) + left.shape, jnp.int16),
            pltpu.SemaphoreType.DMA((7,)),
            pltpu.VMEM((rows_y, WIN, 2 * WIN), jnp.float32),
            pltpu.VMEM((half * WIN, 4 * WIN), jnp.bfloat16),
            pltpu.VMEM((half * WIN, 4 * WIN), jnp.bfloat16),
            pltpu.VMEM((half * WIN, 2 * WIN), jnp.float32),
            pltpu.VMEM((DISP * pad, 2 * WIN), jnp.float32),
        ],
        compiler_params=pltpu.CompilerParams(vmem_limit_bytes=WIDE_LIMIT),
        name="windows",
    )(starts, stats, middle, *bricks, *[jnp.asarray(t) for t in tables])
    result = result.reshape(DISP, DISP, 2 * WIN // (2 * DISP), 2 * DISP)[:, :, :count, :DISP]
    return result.transpose(2, 1, 0, 3).reshape(count, DISP**3)


LANES = 128


def chosen_products(value, member, weights_ref):
    count = weights_ref.shape[1]
    half_count = count // 2
    size = weights_ref.shape[2]
    copies = value.shape[0] // member.shape[0]
    total = None
    for start in range(0, half_count, TERMS):
        picked, tables = [], []
        for j in range(start, min(start + TERMS, half_count)):
            hit = (member == j) | (member == j + half_count)
            hit = jnp.concatenate([hit] * copies, axis=0)
            picked.append(jnp.where(hit, value, jnp.zeros_like(value)))
            tables.append(
                jnp.concatenate([weights_ref[0, j], weights_ref[0, j + half_count]], axis=1)
            )
        term = mul(jnp.concatenate(picked, axis=1), jnp.concatenate(tables, axis=0))
        total = term if total is None else total + term
    upper = jnp.concatenate([member.astype(jnp.float32)] * copies, axis=0) >= half_count
    return jnp.where(upper, total[:, size:], total[:, :size])


def placed_tiles(tile, count):
    columns = lax.broadcasted_iota(jnp.int32, tile.shape, 1).astype(jnp.float32)
    columns = columns.astype(tile.dtype)
    one, zero = jnp.ones_like(tile), jnp.zeros_like(tile)
    parts = [
        jnp.where(tile - start == columns, one, zero) for start in range(0, count, LANES)
    ]
    return jnp.concatenate(parts, axis=1)[:, :count]


def updated(volume, ratio, tile, member, weights_ref):
    placement = placed_tiles(tile, ratio.shape[0])
    spread = mul(placement, ratio).astype(jnp.bfloat16)
    return volume * jnp.exp(chosen_products(spread, member, weights_ref))


def sweep_body(back, forward, volume_ref, *refs):
    refs = list(refs)
    if back:
        ratio_ref, back_tile, back_member, back_weights = refs[:4]
        refs = refs[4:]
    if forward:
        next_row, next_member, next_weights = refs[:3]
        refs = refs[3:]
    volume = volume_ref[...]
    if back:
        volume = updated(volume, ratio_ref[...], back_tile[0], back_member[0], back_weights)
        refs.pop(0)[...] = volume
    if forward:
        (partial_ref,) = refs
        tiles = partial_ref.shape[0]
        projected = chosen_products(volume.astype(jnp.bfloat16), next_member[0], next_weights)
        rows = lax.broadcasted_iota(jnp.int32, (tiles, volume.shape[0]), 0)
        placement = jnp.where(next_row[0] == rows, 1.0, 0.0).astype(jnp.bfloat16)
        value = mul(placement, jnp.concatenate(halves(projected), axis=1))
        size = value.shape[1] // 2
        partial_ref[...] = value[:, :size] + value[:, size:]


def last_body(parity_ref, *refs):
    kept, other, own_ratio, other_ratio, tile, member, weights, volume_out, code_out = refs
    columns, depth = kept.shape
    parity = parity_ref[0]
    pairs = ((parity, kept, own_ratio), (1 - parity, other, other_ratio))
    for e, volume_ref, ratio_ref in pairs:
        volume = updated(volume_ref[...], ratio_ref[...], tile[0], member[0], weights)
        volume_out[e] = volume
        logs = jnp.log(jnp.maximum(volume, 1e-37))
        least = jnp.floor(jnp.min(logs, axis=0, keepdims=True) * GRAIN)
        width = jnp.floor(jnp.max(logs, axis=0, keepdims=True) * GRAIN - least) + 1.0
        rate = (GRAIN * LEVELS) / width
        level = jnp.floor((logs - least / GRAIN) * rate + 0.5) - MIDDLE
        code_out[e, :columns, :] = level.astype(jnp.int32).astype(jnp.int16)
        row = lax.broadcasted_iota(jnp.int32, (SPARE, depth), 0)
        extra = jnp.where(row == 0, least, jnp.where(row == 1, width, 0.0))
        code_out[e, columns:, :] = extra.astype(jnp.int32).astype(jnp.int16)


def taken(value, index):
    shape = (1,) + value.shape[1:]
    return pl.BlockSpec(shape, lambda i: (index,) + (0,) * (len(shape) - 1))


def whole(value):
    return pl.BlockSpec(value.shape, lambda i: (0,) * len(value.shape))


def sweep_step(volume, ratio, columns, weights, weights_turned, tiles, camera, following):
    back, forward = camera is not None, following is not None
    rows, tile_values, members = columns
    operands, specs, shapes = [volume], [whole(volume)], []
    if back:
        operands += [ratio, tile_values, members, weights]
        specs += [whole(ratio)] + [taken(value, camera) for value in operands[-3:]]
        shapes.append(jax.ShapeDtypeStruct(volume.shape, jnp.float32))
    if forward:
        operands += [rows, members, weights_turned]
        specs += [taken(value, following) for value in operands[-3:]]
        shapes.append(jax.ShapeDtypeStruct((tiles, weights.shape[2]), jnp.float32))
    return pl.pallas_call(
        functools.partial(sweep_body, back, forward),
        grid=(1,),
        in_specs=specs,
        out_specs=[whole(value) for value in shapes],
        out_shape=shapes,
        compiler_params=pltpu.CompilerParams(vmem_limit_bytes=LIMIT),
        name="sweep",
    )(*operands)


def last_step(parity, volumes, ratios, columns, weights, camera):
    count, depth = volumes[0].shape
    exposures = len(volumes)
    tables = [columns[1], columns[2], weights]
    shapes = [
        jax.ShapeDtypeStruct((exposures, count, depth), jnp.float32),
        jax.ShapeDtypeStruct((exposures, count + SPARE, depth), jnp.int16),
    ]
    return pl.pallas_call(
        last_body,
        grid=(1,),
        in_specs=[pl.BlockSpec(memory_space=pltpu.SMEM)]
        + [whole(value) for value in (*volumes, *ratios)]
        + [taken(value, camera) for value in tables],
        out_specs=[whole(value) for value in shapes],
        out_shape=shapes,
        compiler_params=pltpu.CompilerParams(vmem_limit_bytes=LIMIT),
        name="last",
    )(parity, *volumes, *ratios, *tables)


def column_tables(target, member):
    shape = target.shape + (LANES,)
    tile_values = jnp.broadcast_to(target.astype(jnp.bfloat16)[..., None], shape)
    members = jnp.broadcast_to(member.astype(jnp.bfloat16)[..., None], shape)
    return target[:, None, :], tile_values, members


def partner_of(count, bit):
    return [(i, i ^ bit) for i in range(count)]


def tree_sum(values):
    while len(values) > 1:
        values = [sum(values[i + 1 : i + 2], values[i]) for i in range(0, len(values), 2)]
    return values[0]


def shared_ratio(total, picture):
    count = lax.axis_size("wide")
    bit = 2
    while bit < count:
        bits = [bit] if 2 * bit >= count else [bit, 2 * bit, 3 * bit]
        arrived = [lax.ppermute(total, "wide", partner_of(count, b)) for b in bits]
        total = tree_sum([total] + arrived)
        bit *= 2 ** ((len(bits) + 1) // 2)
    return (picture - jnp.log(total + 1.0)).astype(jnp.bfloat16)


def reconstructed(initial, images, blocks, lib_index, tile_map):
    count = lax.axis_size("wide")
    own_index = lax.axis_index("wide")
    exposures, brick_x, brick_y, depth = initial.shape
    cameras, tile_rows, tile_cols, pixels = images.shape[1:]
    tile_count = tile_rows * tile_cols
    tiles = count * tile_count
    columns = brick_x * brick_y
    strip = own_index - count // 2 + tile_map // tile_count
    target = strip * tile_count + tile_map % tile_count
    missing = -(-tiles // LANES) * LANES
    target = jnp.where((strip >= 0) & (strip < count), target, missing)
    tables = column_tables(
        target.reshape(cameras, columns), lib_index.reshape(cameras, columns)
    )
    parity = own_index % 2
    pictures = jnp.log(images.reshape(exposures, cameras, tile_count, pixels) + 1.0)
    by_core = jnp.broadcast_to(pictures[None], (count // 2,) + pictures.shape)
    by_core = by_core.reshape((count, cameras, tile_count, pixels))
    gathered = lax.all_to_all(by_core, "wide", split_axis=0, concat_axis=0, tiled=True)
    gathered = gathered.transpose(1, 0, 2, 3).reshape(cameras, tiles, pixels)
    turned = blocks.transpose(0, 1, 3, 2)
    volume = initial.reshape(exposures, columns, depth)
    kept = lax.dynamic_index_in_dim(volume, parity, 0, keepdims=False)
    other = lax.dynamic_index_in_dim(volume, 1 - parity, 0, keepdims=False)
    order = [camera for _ in range(SWEEPS) for camera in range(cameras)]
    step = functools.partial(
        sweep_step, columns=tables, weights=blocks, weights_turned=turned, tiles=tiles
    )

    def swapped(value):
        return lax.ppermute(value, "wide", partner_of(count, 1))

    (sent,) = step(other, None, camera=None, following=order[0])
    (own,) = step(kept, None, camera=None, following=order[0])
    for camera, following in zip(order, order[1:]):
        ratio = shared_ratio(own + swapped(sent), gathered[camera])
        other_ratio = swapped(ratio)
        (kept,) = step(kept, ratio, camera=camera, following=None)
        other, sent = step(other, other_ratio, camera=camera, following=following)
        (own,) = step(kept, None, camera=None, following=following)
    ratio = shared_ratio(own + swapped(sent), gathered[order[-1]])
    return last_step(
        parity.reshape(1), (kept, other), (ratio, swapped(ratio)), tables, blocks, order[-1]
    )


def neighbours(own):
    def shifted(value, axis, step):
        count = lax.axis_size(axis)
        pairs = [(i, i + step) for i in range(count) if 0 <= i + step < count]
        return lax.ppermute(value, axis, pairs)

    near = shifted(own, "narrow", 1)
    right = shifted(own, "wide", -1)
    far = shifted(own, "narrow", -1)
    left = shifted(own, "wide", 1)
    left_near = shifted(near, "wide", 1)
    right_near = shifted(right, "narrow", 1)
    left_far = shifted(far, "wide", 1)
    right_far = shifted(right, "narrow", -1)
    return [left, right, near, far, left_near, left_far, right_near, right_far]


def body(initial, images, blocks, lib_index, tile_map, win_x, win_y, win_z):
    volume, code = reconstructed(initial, images, blocks, lib_index, tile_map)
    starts = jnp.stack([win_x.reshape(-1), win_y.reshape(-1), win_z.reshape(-1)], axis=1)
    correlation = window_correlations(volume, neighbours(code), starts)
    return (volume.reshape(initial.shape), correlation.reshape(1, 1, starts.shape[0], DISP * DISP * DISP))


def solution(mesh):
    placed = (
        P(None, "wide", "narrow", None),
        P(None, None, "wide", "narrow", None),
        P(),
        P(None, "wide", "narrow"),
        P(None, "wide", "narrow"),
        P("wide", "narrow", None),
        P("wide", "narrow", None),
        P("wide", "narrow", None),
    )
    return jax.shard_map(
        body,
        mesh=mesh,
        in_specs=placed,
        out_specs=(P(None, "wide", "narrow", None), P("wide", "narrow", None, None)),
        check_vma=False,
    )
```

```python
import functools
import numpy as np
import jax
import jax.numpy as jnp
from jax import lax
from jax.experimental import pallas as pl
from jax.experimental.pallas import tpu as pltpu
from jax.sharding import PartitionSpec as P

WIN = 64
DISP = 16
SWEEPS = 2
TERMS = 4
LEVELS = 65535.0
MIDDLE = 32768.0
GRAIN = 16.0
SPARE = 16
LIMIT = 24 * 1024 * 1024
WIDE_LIMIT = 60 * 1024 * 1024
GROUPS = 2
THIRD = 1
SPLIT = 3


def split_table(table):
    high = np.asarray(table, np.float32).astype(jnp.bfloat16)
    low = (np.asarray(table, np.float64) - high.astype(np.float64)).astype(np.float32)
    return high, low.astype(jnp.bfloat16)


def window_tables(count):
    half = WIN // 2 + 1
    unit = 2.0 * np.pi / WIN
    index = np.arange(WIN)
    shifts = np.arange(DISP) - DISP // 2
    turn = unit * np.outer(index, index)
    cos_full, sin_full = np.cos(turn), np.sin(turn)
    rows_y = -(-2 * half // 8) * 8
    first = np.zeros((rows_y, WIN))
    first[0 : 2 * half : 2] = cos_full[:half]
    first[1 : 2 * half : 2] = -sin_full[:half]
    high, low = split_table(first)
    table_y = np.concatenate([high, high, low], axis=1)
    second = np.block([[cos_full, sin_full], [-sin_full, cos_full]])
    high, low = split_table(second)
    table_x = np.concatenate([high, high, low], axis=1)
    third = np.zeros((2, 2, WIN, 2, 2, WIN))
    for e in range(2):
        third[0, e, :, e, 0] = cos_full
        third[1, e, :, e, 0] = sin_full
        third[0, e, :, e, 1] = -sin_full
        third[1, e, :, e, 1] = cos_full
    high, low = split_table(third.reshape(4 * WIN, 4 * WIN))
    table_z = np.concatenate([high, high, low], axis=0)
    part = unit * np.outer(index, shifts)
    cos_part, sin_part = np.cos(part), np.sin(part)
    fourth = np.zeros((4, WIN, 2 * WIN))
    fourth[..., :DISP] = np.stack([cos_part, cos_part, -sin_part, sin_part])
    fourth[..., DISP : 2 * DISP] = np.stack([sin_part, sin_part, cos_part, -cos_part])
    fourth = fourth.reshape(4 * WIN, 2 * WIN)
    shifted = np.stack([np.roll(fourth, w * 2 * DISP, axis=1) for w in range(count)])
    high, low = split_table(shifted)
    table_iz = np.concatenate([high, high, low], axis=1)
    high, low = split_table(np.concatenate([cos_part.T, sin_part.T], axis=1))
    table_ix = np.concatenate([high, high, low], axis=1)
    weight = np.full(half, 2.0)
    weight[0] = weight[-1] = 1.0
    pad = -(-half // 16) * 16
    last = np.zeros((2 * DISP, pad))
    last[:DISP, :half] = cos_part.T[:, :half] * weight
    last[DISP:, :half] = sin_part.T[:, :half] * weight
    high, low = split_table(last)
    table_iy = np.concatenate([high, high, low], axis=1)
    return table_y, table_x, table_z, table_iz, table_ix, table_iy


def halves(value):
    high = value.astype(jnp.bfloat16)
    low = (value - high.astype(jnp.float32)).astype(jnp.bfloat16)
    return high, low


def stacked(value):
    high, low = halves(value)
    return jnp.concatenate([high, low, high], axis=0)


def mul(left, right):
    return jnp.dot(left, right, preferred_element_type=jnp.float32)


def decode(level_ref, target_ref):
    exposures, columns = target_ref.shape[:2]
    for e in range(exposures):
        scale = level_ref[e, columns:, :].astype(jnp.int32).astype(jnp.float32)
        least, width = scale[:1] / GRAIN, scale[1:2]
        step = width / (GRAIN * LEVELS)
        base = least + MIDDLE * step
        present = jnp.where(width > 0.0, 1.0, 0.0)
        for start in range(0, columns, columns // 4):
            place = slice(start, start + columns // 4)
            level = level_ref[e, place, :].astype(jnp.int32).astype(jnp.float32)
            target_ref[e, place, :] = jnp.exp(level * step + base) * present


def first_stage(ext, brick_of, start, mean, table, spectrum_ref):
    half_win = WIN // 2
    _, sy, sz = start
    lane = lax.broadcasted_iota(jnp.int32, (WIN, 2 * WIN), 1)
    row = lax.broadcasted_iota(jnp.int32, (half_win, 2 * WIN), 0)
    left_lane = lane < WIN
    keep = (left_lane & (lane >= sz)) | (~left_lane & (lane < sz + WIN))
    below = row >= sy

    def fold(x):
        brick = brick_of(x)
        inner = pl.ds(pl.multiple_of(x * half_win, half_win), half_win)
        values = []
        for e in range(2):
            low, high = ext[brick, e, inner], ext[brick + 2, e, inner]
            same = ext[brick + 1, e, inner]
            values.append(jnp.concatenate([jnp.where(below, low, high), same], axis=0))
        stay = jnp.where(left_lane, values[0], values[1])
        move = jnp.where(left_lane, values[1], values[0])
        return jnp.where(keep, stay, pltpu.roll(move, WIN, 1)) - mean

    def one_group(i, sums):
        total, square = sums
        for g in range(GROUPS):
            begin = (i * GROUPS + g) * 8
            results = []
            for j in range(0, 8, 2):
                values = [fold(begin + j + k) for k in range(2)]
                for value in values:
                    total = total + value
                    square = square + value * value
                result = mul(table, stacked(jnp.concatenate(values, axis=1)))
                results += [result[:, : 2 * WIN], result[:, 2 * WIN :]]
            spectrum_ref[:, pl.ds(pl.multiple_of(begin, 8), 8), :] = jnp.swapaxes(
                jnp.stack(results), 0, 1
            )
        return total, square

    zero = jnp.zeros((WIN, 2 * WIN), jnp.float32)
    total, square = lax.fori_loop(0, half_win // (8 * GROUPS), one_group, (zero, zero))
    return [jnp.sum(value, axis=0, keepdims=True) for value in (total, square)]


def by_exposure(value):
    left = lax.broadcasted_iota(jnp.int32, value.shape, 1) < WIN
    return (
        jnp.sum(jnp.where(left, value, 0.0), axis=1, keepdims=True),
        jnp.sum(jnp.where(left, 0.0, value), axis=1, keepdims=True),
    )


def middle_body(count, starts, own, near, far, t_y, spectrum_out, stats_out, ext, levels, sems):
    copies = [
        pltpu.make_async_copy(source, target, sems.at[i])
        for i, (source, target) in enumerate(
            [(own, ext.at[1]), (near, levels.at[0]), (far, levels.at[1])]
        )
    ]
    for copy in copies:
        copy.start()
    for copy in copies:
        copy.wait()
    decode(levels.at[0], ext.at[0])
    decode(levels.at[1], ext.at[2])
    exposures, columns, depth = ext.shape[1:]
    sums = [jnp.sum(ext[1, e], axis=0, keepdims=True) for e in range(exposures)]
    lane = lax.broadcasted_iota(jnp.int32, (1, depth), 1)

    def one_window(w, done):
        start = [starts[w, n] for n in range(3)]
        inside = (lane >= start[2]) & (lane < start[2] + WIN)
        means = [
            jnp.sum(jnp.where(inside, value, 0.0), axis=1, keepdims=True) / (columns * WIN)
            for value in sums
        ]
        mean = jnp.where(lane < WIN, means[0], means[1])
        total, square = first_stage(
            ext, lambda x: 0, start, mean, t_y[...], spectrum_out.at[w]
        )
        spare = jnp.zeros((5, depth), jnp.float32)
        stats_out[w] = jnp.concatenate([mean, total, square, spare], axis=0)
        return done

    lax.fori_loop(0, count, one_window, 0)


def window_body(count, starts, stats, *refs):
    middle, left, right, left_near, left_far, right_near, right_far = refs[:7]
    table_sources, out = refs[7:13], refs[13]
    ext, levels, sems, spectrum, high_ref, low_ref, product, turned = refs[14:22]
    t_y, t_x, t_z, t_iz, t_ix, t_iy = refs[22:]
    half = WIN // 2 + 1
    pad = t_iy.shape[1] // 3
    sources = [left_near, left, left_far, right_near, right, right_far]
    copies = [
        pltpu.make_async_copy(source, levels.at[i], sems.at[i])
        for i, source in enumerate(sources)
    ]

    loads = [
        pltpu.make_async_copy(source, target, sems.at[len(sources) + 1 + i])
        for i, (source, target) in enumerate(zip(table_sources, refs[22:]))
    ]

    def middle_copy(w):
        target = spectrum.at[:, pl.ds(WIN // 2, WIN // 2), :]
        return pltpu.make_async_copy(middle.at[w], target, sems.at[len(sources)])

    for copy in copies + loads:
        copy.start()
    middle_copy(0).start()
    product[...] = jnp.zeros_like(product)
    turned[...] = jnp.zeros_like(turned)
    for copy in copies:
        copy.wait()

    def decode_one(i, done):
        decode(levels.at[i], ext.at[i])
        return done

    lax.fori_loop(0, len(sources), decode_one, 0)
    for copy in loads:
        copy.wait()
    lane = lax.broadcasted_iota(jnp.int32, (WIN, 2 * WIN), 1)

    def one_window(w, carry):
        start = [starts[w, n] for n in range(3)]
        known = stats[w]
        total, square = first_stage(
            ext,
            lambda x: jnp.where(x >= start[0], 0, 3),
            start,
            known[:1],
            t_y[...],
            spectrum,
        )
        scale = 1.0 / WIN**3
        totals, squares = by_exposure(total + known[1:2]), by_exposure(square + known[2:3])
        powers = [
            square * scale - (total * scale) * (total * scale)
            for total, square in zip(totals, squares)
        ]
        norm = jnp.sqrt(powers[0] + 1e-06) * jnp.sqrt(powers[1] + 1e-06)
        factor = 1.0 / (WIN**3 * WIN**1.5) / norm
        middle_copy(w).wait()

        def second(i, done):
            for j in range(0, 11, 2):
                width = min(2, 11 - j)
                k = i * 11 + j
                values = [
                    spectrum[pl.ds(2 * (k + n), 2)].reshape(2 * WIN, 2 * WIN) for n in range(width)
                ]
                result = mul(t_x[...], stacked(jnp.concatenate(values, axis=1)))
                for n in range(width):
                    part = result[:, 2 * WIN * n : 2 * WIN * (n + 1)]
                    part = jnp.concatenate([part[:WIN], part[WIN:]], axis=1)
                    place = pl.ds(pl.multiple_of((k + n) * WIN, WIN), WIN)
                    high_ref[place, :], low_ref[place, :] = halves(part)
            return done

        lax.fori_loop(0, half // 11, second, 0)

        @pl.when(w + 1 < count)
        def _():
            middle_copy(w + 1).start()

        block = half * WIN // (THIRD * SPLIT)

        def third(i, done):
            for g in range(SPLIT):
                place = pl.ds(pl.multiple_of((i * SPLIT + g) * block, block), block)
                high, low = high_ref[place, :], low_ref[place, :]
                value = mul(jnp.concatenate([high, low, high], axis=1), t_z[...])
                one, two = value[:, : 2 * WIN] * factor, value[:, 2 * WIN :]
                if g == 0:
                    row = lax.broadcasted_iota(jnp.int32, one.shape, 0)
                    column = lax.broadcasted_iota(jnp.int32, one.shape, 1)
                    one = jnp.where((i * block + row == 0) & (column % WIN == 0), 0.0, one)
                cross = jnp.concatenate([one * two, one * pltpu.roll(two, WIN, 1)], axis=1)
                high, low = halves(cross)
                product[place, :] += mul(jnp.concatenate([high, low, high], axis=1), t_iz[w])
            return done

        lax.fori_loop(0, THIRD, third, 0)
        return carry

    lax.fori_loop(0, count, one_window, 0)

    real_lane = lane % (2 * DISP) < DISP

    def fifth(i, done):
        for j in range(11):
            k = i * 11 + j
            value = product[pl.ds(pl.multiple_of(k * WIN, WIN), WIN), :]
            turn = jnp.where(
                real_lane, -pltpu.roll(value, 2 * WIN - DISP, 1), pltpu.roll(value, DISP, 1)
            )
            value = jnp.concatenate([value, turn], axis=0)
            turned[pl.ds(k, DISP, stride=pad), :] = mul(t_ix[...], stacked(value))
        return done

    lax.fori_loop(0, half // 11, fifth, 0)
    for d in range(DISP):
        value = mul(t_iy[...], stacked(turned[d * pad : (d + 1) * pad, :]))
        out[:, d * 2 * WIN : (d + 1) * 2 * WIN] = value[:DISP] - pltpu.roll(
            value[DISP:], 2 * WIN - DISP, 1
        )


def middle_spectra(own, near, far, starts):
    count = starts.shape[0]
    table = window_tables(count)[0]
    vmem = pl.BlockSpec(memory_space=pltpu.VMEM)
    anywhere = pl.BlockSpec(memory_space=pltpu.HBM)
    return pl.pallas_call(
        functools.partial(middle_body, count),
        out_shape=[
            jax.ShapeDtypeStruct((count, table.shape[0], WIN // 2, 2 * WIN), jnp.float32),
            jax.ShapeDtypeStruct((count, 8, 2 * WIN), jnp.float32),
        ],
        in_specs=[pl.BlockSpec(memory_space=pltpu.SMEM), anywhere, anywhere, anywhere, vmem],
        out_specs=[vmem, vmem],
        scratch_shapes=[
            pltpu.VMEM((3,) + own.shape, jnp.float32),
            pltpu.VMEM((2,) + near.shape, jnp.int16),
            pltpu.SemaphoreType.DMA((3,)),
        ],
        compiler_params=pltpu.CompilerParams(vmem_limit_bytes=LIMIT),
        name="middle",
    )(starts, own, near, far, jnp.asarray(table))


def window_correlations(own, bricks, starts):
    left, right, near, far, *corners = bricks
    middle, stats = middle_spectra(own, near, far, starts)
    bricks = [left, right, *corners]
    count = starts.shape[0]
    tables = window_tables(count)
    half = WIN // 2 + 1
    rows_y = tables[0].shape[0]
    pad = tables[5].shape[1] // 3
    vmem = pl.BlockSpec(memory_space=pltpu.VMEM)
    result = pl.pallas_call(
        functools.partial(window_body, count),
        out_shape=jax.ShapeDtypeStruct((DISP, DISP * 2 * WIN), jnp.float32),
        in_specs=[pl.BlockSpec(memory_space=pltpu.SMEM), vmem]
        + [pl.BlockSpec(memory_space=pltpu.HBM)] * 13,
        out_specs=vmem,
        scratch_shapes=[
            pltpu.VMEM((6,) + own.shape, jnp.float32),
            pltpu.VMEM((6,) + left.shape, jnp.int16),
            pltpu.SemaphoreType.DMA((13,)),
            pltpu.VMEM((rows_y, WIN, 2 * WIN), jnp.float32),
            pltpu.VMEM((half * WIN, 4 * WIN), jnp.bfloat16),
            pltpu.VMEM((half * WIN, 4 * WIN), jnp.bfloat16),
            pltpu.VMEM((half * WIN, 2 * WIN), jnp.float32),
            pltpu.VMEM((DISP * pad, 2 * WIN), jnp.float32),
        ]
        + [pltpu.VMEM(table.shape, jnp.bfloat16) for table in tables],
        compiler_params=pltpu.CompilerParams(vmem_limit_bytes=WIDE_LIMIT),
        name="windows",
    )(starts, stats, middle, *bricks, *[jnp.asarray(t) for t in tables])
    result = result.reshape(DISP, DISP, 2 * WIN // (2 * DISP), 2 * DISP)[:, :, :count, :DISP]
    return result.transpose(2, 1, 0, 3).reshape(count, DISP**3)


LANES = 128


def chosen_products(value, member, weights_ref):
    count = weights_ref.shape[1]
    half_count = count // 2
    size = weights_ref.shape[2]
    copies = value.shape[0] // member.shape[0]
    total = None
    for start in range(0, half_count, TERMS):
        picked, tables = [], []
        for j in range(start, min(start + TERMS, half_count)):
            hit = (member == j) | (member == j + half_count)
            hit = jnp.concatenate([hit] * copies, axis=0)
            picked.append(jnp.where(hit, value, jnp.zeros_like(value)))
            tables.append(
                jnp.concatenate([weights_ref[0, j], weights_ref[0, j + half_count]], axis=1)
            )
        term = mul(jnp.concatenate(picked, axis=1), jnp.concatenate(tables, axis=0))
        total = term if total is None else total + term
    upper = jnp.concatenate([member.astype(jnp.float32)] * copies, axis=0) >= half_count
    return jnp.where(upper, total[:, size:], total[:, :size])


def placed_tiles(tile, count):
    columns = lax.broadcasted_iota(jnp.int32, tile.shape, 1).astype(jnp.float32)
    columns = columns.astype(tile.dtype)
    one, zero = jnp.ones_like(tile), jnp.zeros_like(tile)
    parts = [
        jnp.where(tile - start == columns, one, zero) for start in range(0, count, LANES)
    ]
    return jnp.concatenate(parts, axis=1)[:, :count]


def updated(volume, ratio, tile, member, weights_ref):
    placement = placed_tiles(tile, ratio.shape[0])
    spread = mul(placement, ratio).astype(jnp.bfloat16)
    return volume * jnp.exp(chosen_products(spread, member, weights_ref))


def sweep_body(back, forward, volume_ref, *refs):
    refs = list(refs)
    if back:
        ratio_ref, back_tile, back_member, back_weights = refs[:4]
        refs = refs[4:]
    if forward:
        next_row, next_member, next_weights = refs[:3]
        refs = refs[3:]
    volume = volume_ref[...]
    if back:
        volume = updated(volume, ratio_ref[...], back_tile[0], back_member[0], back_weights)
        refs.pop(0)[...] = volume
    if forward:
        (partial_ref,) = refs
        tiles = partial_ref.shape[0]
        projected = chosen_products(volume.astype(jnp.bfloat16), next_member[0], next_weights)
        rows = lax.broadcasted_iota(jnp.int32, (tiles, volume.shape[0]), 0)
        placement = jnp.where(next_row[0] == rows, 1.0, 0.0).astype(jnp.bfloat16)
        value = mul(placement, jnp.concatenate(halves(projected), axis=1))
        size = value.shape[1] // 2
        partial_ref[...] = value[:, :size] + value[:, size:]


def last_body(parity_ref, *refs):
    kept, other, other_ratio, tile, member, weights, volume_out, code_out = refs
    columns, depth = kept.shape
    parity = parity_ref[0]
    for e in (parity, 1 - parity):
        if e is parity:
            volume = kept[...]
        else:
            volume = updated(other[...], other_ratio[...], tile[0], member[0], weights)
        volume_out[e] = volume
        logs = jnp.log(jnp.maximum(volume, 1e-37))
        least = jnp.floor(jnp.min(logs, axis=0, keepdims=True) * GRAIN)
        width = jnp.floor(jnp.max(logs, axis=0, keepdims=True) * GRAIN - least) + 1.0
        rate = (GRAIN * LEVELS) / width
        level = jnp.floor((logs - least / GRAIN) * rate + 0.5) - MIDDLE
        code_out[e, :columns, :] = level.astype(jnp.int32).astype(jnp.int16)
        row = lax.broadcasted_iota(jnp.int32, (SPARE, depth), 0)
        extra = jnp.where(row == 0, least, jnp.where(row == 1, width, 0.0))
        code_out[e, columns:, :] = extra.astype(jnp.int32).astype(jnp.int16)


def taken(value, index):
    shape = (1,) + value.shape[1:]
    return pl.BlockSpec(shape, lambda i: (index,) + (0,) * (len(shape) - 1))


def whole(value):
    return pl.BlockSpec(value.shape, lambda i: (0,) * len(value.shape))


def sweep_step(volume, ratio, columns, weights, weights_turned, tiles, camera, following):
    back, forward = camera is not None, following is not None
    rows, tile_values, members = columns
    operands, specs, shapes = [volume], [whole(volume)], []
    if back:
        operands += [ratio, tile_values, members, weights]
        specs += [whole(ratio)] + [taken(value, camera) for value in operands[-3:]]
        shapes.append(jax.ShapeDtypeStruct(volume.shape, jnp.float32))
    if forward:
        operands += [rows, members, weights_turned]
        specs += [taken(value, following) for value in operands[-3:]]
        shapes.append(jax.ShapeDtypeStruct((tiles, weights.shape[2]), jnp.float32))
    return pl.pallas_call(
        functools.partial(sweep_body, back, forward),
        grid=(1,),
        in_specs=specs,
        out_specs=[whole(value) for value in shapes],
        out_shape=shapes,
        compiler_params=pltpu.CompilerParams(vmem_limit_bytes=LIMIT),
        name="sweep",
    )(*operands)


def last_step(parity, volumes, ratio, columns, weights, camera):
    count, depth = volumes[0].shape
    exposures = len(volumes)
    tables = [columns[1], columns[2], weights]
    shapes = [
        jax.ShapeDtypeStruct((exposures, count, depth), jnp.float32),
        jax.ShapeDtypeStruct((exposures, count + SPARE, depth), jnp.int16),
    ]
    return pl.pallas_call(
        last_body,
        grid=(1,),
        in_specs=[pl.BlockSpec(memory_space=pltpu.SMEM)]
        + [whole(value) for value in (*volumes, ratio)]
        + [taken(value, camera) for value in tables],
        out_specs=[whole(value) for value in shapes],
        out_shape=shapes,
        compiler_params=pltpu.CompilerParams(vmem_limit_bytes=LIMIT),
        name="last",
    )(parity, *volumes, ratio, *tables)


def column_tables(target, member):
    shape = target.shape + (LANES,)
    tile_values = jnp.broadcast_to(target.astype(jnp.bfloat16)[..., None], shape)
    members = jnp.broadcast_to(member.astype(jnp.bfloat16)[..., None], shape)
    return target[:, None, :], tile_values, members


def partner_of(count, bit):
    return [(i, i ^ bit) for i in range(count)]


def tree_sum(values):
    while len(values) > 1:
        values = [sum(values[i + 1 : i + 2], values[i]) for i in range(0, len(values), 2)]
    return values[0]


def shared_ratio(total, picture):
    count = lax.axis_size("wide")
    bit = 2
    while bit < count:
        bits = [bit] if 2 * bit >= count else [bit, 2 * bit, 3 * bit]
        arrived = [lax.ppermute(total, "wide", partner_of(count, b)) for b in bits]
        total = tree_sum([total] + arrived)
        bit *= 2 ** ((len(bits) + 1) // 2)
    return (picture - jnp.log(total + 1.0)).astype(jnp.bfloat16)


def reconstructed(initial, images, blocks, lib_index, tile_map):
    count = lax.axis_size("wide")
    own_index = lax.axis_index("wide")
    exposures, brick_x, brick_y, depth = initial.shape
    cameras, tile_rows, tile_cols, pixels = images.shape[1:]
    tile_count = tile_rows * tile_cols
    tiles = count * tile_count
    columns = brick_x * brick_y
    strip = own_index - count // 2 + tile_map // tile_count
    target = strip * tile_count + tile_map % tile_count
    missing = -(-tiles // LANES) * LANES
    target = jnp.where((strip >= 0) & (strip < count), target, missing)
    tables = column_tables(
        target.reshape(cameras, columns), lib_index.reshape(cameras, columns)
    )
    parity = own_index % 2
    pictures = jnp.log(images.reshape(exposures, cameras, tile_count, pixels) + 1.0)
    by_core = jnp.broadcast_to(pictures[None], (count // 2,) + pictures.shape)
    by_core = by_core.reshape((count, cameras, tile_count, pixels))
    gathered = lax.all_to_all(by_core, "wide", split_axis=0, concat_axis=0, tiled=True)
    gathered = gathered.transpose(1, 0, 2, 3).reshape(cameras, tiles, pixels)
    turned = blocks.transpose(0, 1, 3, 2)
    volume = initial.reshape(exposures, columns, depth)
    kept = lax.dynamic_index_in_dim(volume, parity, 0, keepdims=False)
    other = lax.dynamic_index_in_dim(volume, 1 - parity, 0, keepdims=False)
    order = [camera for _ in range(SWEEPS) for camera in range(cameras)]
    step = functools.partial(
        sweep_step, columns=tables, weights=blocks, weights_turned=turned, tiles=tiles
    )

    def swapped(value):
        return lax.ppermute(value, "wide", partner_of(count, 1))

    (sent,) = step(other, None, camera=None, following=order[0])
    (own,) = step(kept, None, camera=None, following=order[0])
    for camera, following in zip(order, order[1:]):
        ratio = shared_ratio(own + swapped(sent), gathered[camera])
        other_ratio = swapped(ratio)
        (kept,) = step(kept, ratio, camera=camera, following=None)
        other, sent = step(other, other_ratio, camera=camera, following=following)
        (own,) = step(kept, None, camera=None, following=following)
    ratio = shared_ratio(own + swapped(sent), gathered[order[-1]])
    other_ratio = swapped(ratio)
    (kept,) = step(kept, ratio, camera=order[-1], following=None)
    return last_step(parity.reshape(1), (kept, other), other_ratio, tables, blocks, order[-1])


def neighbours(own):
    def shifted(value, axis, step):
        count = lax.axis_size(axis)
        pairs = [(i, i + step) for i in range(count) if 0 <= i + step < count]
        return lax.ppermute(value, axis, pairs)

    near = shifted(own, "narrow", 1)
    right = shifted(own, "wide", -1)
    far = shifted(own, "narrow", -1)
    left = shifted(own, "wide", 1)
    left_near = shifted(near, "wide", 1)
    right_near = shifted(right, "narrow", 1)
    left_far = shifted(far, "wide", 1)
    right_far = shifted(right, "narrow", -1)
    return [left, right, near, far, left_near, left_far, right_near, right_far]


def body(initial, images, blocks, lib_index, tile_map, win_x, win_y, win_z):
    volume, code = reconstructed(initial, images, blocks, lib_index, tile_map)
    starts = jnp.stack([win_x.reshape(-1), win_y.reshape(-1), win_z.reshape(-1)], axis=1)
    correlation = window_correlations(volume, neighbours(code), starts)
    return (volume.reshape(initial.shape), correlation.reshape(1, 1, starts.shape[0], DISP * DISP * DISP))


def solution(mesh):
    placed = (
        P(None, "wide", "narrow", None),
        P(None, None, "wide", "narrow", None),
        P(),
        P(None, "wide", "narrow"),
        P(None, "wide", "narrow"),
        P("wide", "narrow", None),
        P("wide", "narrow", None),
        P("wide", "narrow", None),
    )
    return jax.shard_map(
        body,
        mesh=mesh,
        in_specs=placed,
        out_specs=(P(None, "wide", "narrow", None), P("wide", "narrow", None, None)),
        check_vma=False,
    )
```
